256 devices in a mesh: pb: 16 (over x, y_hi, core), ka: 8 (over z), ga: 2 (over y_lo).
Axes of the slice: x: 4, y: 4 (y_hi: 2, y_lo: 2; y = y_hi * 2 + y_lo), z: 8, core: 2. Of those that a mesh axis runs over, the one named last changes fastest.
Arguments:
- queries: bfloat16 [16, 2048, 768], P(None, 'pb', 'ga'), may hold values from -6 to 6
- comp_keys: bfloat16 [8192, 768], P(('ka', 'pb'), 'ga'), may hold values from -6 to 6
- comp_values: bfloat16 [8192, 512], P(('ka', 'pb'), 'ga'), may hold values from -6 to 6
- outputs: bfloat16 [16, 2048, 512], P(None, 'pb', 'ga'), may hold values from -1.1953125 to 1.1953125
- grad_out: bfloat16 [16, 2048, 512], P(None, 'pb', 'ga'), may hold values from -300 to 300
- log_sums: float32 [4, 16, 2048], P('ga', None, 'pb'), may hold values from 7 to 10
- visible: int32 [32, 8192], P('pb', 'ka'), may hold values from 0 to 1, as said below
Outputs:
- grad_queries: float32 [16, 2048, 768], P('ka', 'pb', 'ga')
- grad_keys: float32 [8192, 768], P(('ka', 'pb'), 'ga')
- grad_values: float32 [8192, 512], P(('ka', 'pb'), 'ga')
The draws below stay inside these ranges and needn't reach their ends.
Inputs may be any that keep to these rules, and one draw needn't show every extreme that they name: The queries are the last 2048 positions of a sequence of 131072 positions, and compressed key j covers positions 16 * j to 16 * j + 31. visible[b, j] is 1 exactly when key j ends before the first position of query block b and starts no earlier than the start of the document that holds that position; the sequence is packed from a few documents.
All inputs are finite; a program needn't handle non-finite values.
Results may differ from the reference program's by a relative error of at most 0.0029.
Values may be sent and summed in bfloat16 or wider, within the bound.
No kernel may reach another device: no remote copies, remote signals or barrier semaphores. Data moves between devices by JAX's collectives and lax.ppermute only.
A program may use at most 64 MiB of HBM per device.

```python
import math
import jax
import jax.numpy as jnp
from jax import lax

G = 4
HG = 16
DK = 192
DV = 128
QBLK = 64
STRIDE = 16
SPAN = 32
NQ = 2048
KEYS = 8192
NQB = 32


def draw_visible(key, part):
    positions = KEYS * STRIDE
    starts = jax.random.randint(jax.random.fold_in(key, 11), (2,), 0, positions)
    window_start = positions - NQB * QBLK
    block_first = window_start + jnp.arange(NQB, dtype=jnp.int32) * QBLK
    key_first = jnp.arange(KEYS, dtype=jnp.int32) * STRIDE
    key_last = key_first + SPAN - 1
    doc_start = jnp.max(jnp.where(starts[None, :] <= block_first[:, None], starts[None, :], 0), axis=1)
    drawn = (key_last[None, :] < block_first[:, None]) & (key_first[None, :] >= doc_start[:, None])
    return drawn.astype(jnp.int32)


def block_scale(key, dims, pieces, smallest, high):
    def one(dim, blocks):
        heights = jax.random.uniform(jax.random.fold_in(jax.random.fold_in(key, 6), dim), (blocks,), jnp.float32, smallest / len(pieces), high / len(pieces))
        return jnp.repeat(jnp.exp(heights), dims[dim] // blocks).reshape((-1,) + (1,) * (len(dims) - dim - 1))

    level = one(*pieces[0])
    for cut in pieces[1:]:
        level = level * one(*cut)
    return level


def scatter_about(own_key, shape, spread, bound, pieces=(), kind=jnp.bfloat16):
    entries = spread * jax.random.normal(own_key, shape, jnp.float32)
    if pieces:
        entries = entries * block_scale(own_key, shape, pieces, -0.22, 0.18)
    return jnp.clip(entries, -bound, bound).astype(kind)


def setup_inputs(seed: int = 0) -> dict:
    key_list = jax.random.split(jax.random.key(seed), 8)
    queries = scatter_about(key_list[0], (HG, NQ, G * DK), 1.0, 6.0, ((1, 16), (2, 2)))
    comp_keys = scatter_about(key_list[1], (KEYS, G * DK), 1.0, 6.0, ((0, 128), (1, 2)))
    comp_values = scatter_about(key_list[2], (KEYS, G * DV), 1.0, 6.0, ((0, 128), (1, 2)))
    outputs = scatter_about(key_list[3], (HG, NQ, G * DV), 0.2, 1.1953125, ((1, 16), (2, 2)))
    grad_out = scatter_about(key_list[4], (HG, NQ, G * DV), 50.0, 300.0, ((1, 16), (2, 2)))
    log_sums = jnp.clip(7.0 + 3.0 * jax.random.uniform(key_list[5], (G, HG, NQ), jnp.float32) ** block_scale(key_list[5], (G, HG, NQ), ((0, 2), (2, 16)), -0.2, 0.2), 7.0, 10.0)
    visible = draw_visible(jax.random.fold_in(key_list[7], 71), 0)
    return dict(queries=queries, comp_keys=comp_keys, comp_values=comp_values, outputs=outputs, grad_out=grad_out, log_sums=log_sums, visible=visible)


def reference(queries, comp_keys, comp_values, outputs, grad_out, log_sums, visible):
    softmax_scale = 1.0 / math.sqrt(DK)
    block_rows = min(512, KEYS)
    blocks = KEYS // block_rows
    query_total = queries.shape[1]
    mask_blocks = visible.reshape(NQB, blocks, block_rows).transpose(1, 0, 2)
    grads_query = []
    grads_key = []
    grads_value = []
    for group_index in range(G):
        query_group = queries[:, :, group_index * DK:(group_index + 1) * DK].astype(jnp.float32)
        grad_group = grad_out[:, :, group_index * DV:(group_index + 1) * DV].astype(jnp.float32)
        out_group = outputs[:, :, group_index * DV:(group_index + 1) * DV].astype(jnp.float32)
        row_delta = lax.optimization_barrier(jnp.sum(grad_group * out_group, axis=2))
        row_lse = log_sums[group_index]
        key_group = comp_keys[:, group_index * DK:(group_index + 1) * DK].reshape(blocks, block_rows, DK)
        value_group = comp_values[:, group_index * DV:(group_index + 1) * DV].reshape(blocks, block_rows, DV)

        def advance(running, inputs, query_group=query_group, grad_group=grad_group, row_delta=row_delta, row_lse=row_lse):
            key_block, value_block, mask_block = inputs
            key_float = key_block.astype(jnp.float32)
            scores = jnp.einsum('hqd,kd->hqk', query_group, key_float) * softmax_scale
            weights = jnp.repeat(mask_block, QBLK, axis=0).astype(jnp.float32)
            probs_full = jnp.exp(scores - row_lse[:, :, None]) * weights[None]
            probs_low = lax.optimization_barrier(probs_full.astype(jnp.bfloat16)).astype(jnp.float32)
            grad_probs = jnp.einsum('hqd,kd->hqk', grad_group, value_block.astype(jnp.float32))
            grad_scores = probs_full * (grad_probs - row_delta[:, :, None])
            grad_low = lax.optimization_barrier(grad_scores.astype(jnp.bfloat16)).astype(jnp.float32)
            value_grad = jnp.einsum('hqk,hqd->kd', probs_low, grad_group)
            key_grad = jnp.einsum('hqk,hqd->kd', grad_low, query_group) * softmax_scale
            query_grad = jnp.einsum('hqk,kd->hqd', grad_low, key_float) * softmax_scale
            return (running + query_grad, (key_grad, value_grad))
        initial = jnp.zeros((HG, query_total, DK), jnp.float32)
        query_sum, (key_parts, value_parts) = lax.scan(advance, initial, (key_group, value_group, mask_blocks))
        grads_query.append(query_sum)
        grads_key.append(key_parts.reshape(KEYS, DK))
        grads_value.append(value_parts.reshape(KEYS, DV))
    return (jnp.concatenate(grads_query, axis=2), jnp.concatenate(grads_key, axis=1), jnp.concatenate(grads_value, axis=1))
```

```python
import math

import jax
import jax.numpy as jnp
from jax import lax
from jax.experimental import pallas as pl
from jax.experimental.pallas import tpu as pltpu
from jax.sharding import PartitionSpec as P

DK = 192
DV = 128
QBLK = 64
LANES = 128
WIN = 256
SCALE = 1.0 / math.sqrt(DK)
LOG2E = math.log2(math.e)
KEY_TILE = 256
HEADS = 4


def grad_kernel(group, q_ref, do_ref, own_ref, par_ref, lse_ref, delta_ref, mask_ref,
                dqt_ref, own_out, par_out, kz, kt, acc_k, acc_v):
    heads = q_ref.shape[0]
    half = own_ref.shape[0]
    lo = group * LANES
    vlo = 3 * LANES + group * LANES
    lane = lax.broadcasted_iota(jnp.int32, (KEY_TILE, WIN), 1)
    keep = (lane < DK) if group == 0 else (lane >= WIN - DK)
    tiles = []
    for side, ref in enumerate((own_ref, par_ref)):
        for t in range(half // KEY_TILE):
            tiles.append((ref, t * KEY_TILE, side * half + t * KEY_TILE))
    for ref, at, row in tiles:
        k = jnp.where(keep, ref[at:at + KEY_TILE, lo:lo + WIN], jnp.zeros((), jnp.bfloat16))
        kz[row:row + KEY_TILE, :] = k
        kt[:, row:row + KEY_TILE] = k.T
    acc_k[...] = jnp.zeros_like(acc_k)
    acc_v[...] = jnp.zeros_like(acc_v)
    first = 0 if group == 0 else WIN - DK
    rows = HEADS * q_ref.shape[1]
    nt = (((1,), (1,)), ((), ()))
    nn = (((1,), (0,)), ((), ()))
    f32 = jnp.float32

    def dot(a, b, dims):
        return lax.dot_general(a, b, dims, preferred_element_type=f32)

    def chunk(i, carry):
        h = i * HEADS
        q = q_ref[pl.ds(h, HEADS), :, lo:lo + WIN].reshape(rows, WIN)
        do = do_ref[pl.ds(h, HEADS), :, lo:lo + DV].reshape(rows, DV)
        lse = jnp.concatenate([lse_ref[pl.ds(h + j, 1), :] for j in range(HEADS)], axis=1) * LOG2E
        delta = jnp.concatenate([delta_ref[pl.ds(h + j, 1), :] for j in range(HEADS)], axis=1)
        dqt = jnp.zeros((DK, rows), f32)
        for ref, at, row in tiles:
            s = dot(kz[row:row + KEY_TILE, :], q, nt)
            dp = dot(ref[at:at + KEY_TILE, vlo:vlo + DV], do, nt)
            m = mask_ref[row:row + KEY_TILE, :]
            m = jnp.concatenate([m] * HEADS, axis=1)
            p = jnp.exp2(s * (SCALE * LOG2E) - lse) * m
            ds = (p * (dp - delta)).astype(jnp.bfloat16)
            p = p.astype(jnp.bfloat16)
            acc_v[row:row + KEY_TILE, :] += dot(p, do, nn)
            acc_k[row:row + KEY_TILE, :] += dot(ds, q, nn)
            dqt = dqt + dot(kt[first:first + DK, row:row + KEY_TILE], ds, nn)
        dqt = (dqt * SCALE).astype(jnp.bfloat16)
        for j in range(HEADS):
            dqt_ref[h + j, :, :] = dqt[:, j * LANES:(j + 1) * LANES]
        return carry

    lax.fori_loop(0, heads // HEADS, chunk, 0)
    own_out[:, :WIN] = acc_k[:half, :] * SCALE
    own_out[:, WIN:] = acc_v[:half, :]
    par_out[:, :WIN] = (acc_k[half:, :] * SCALE).astype(jnp.bfloat16)
    par_out[:, WIN:] = acc_v[half:, :].astype(jnp.bfloat16)


def group_grads(group, q, do, own, par, lse, delta, mask):
    heads, count, _ = q.shape
    half = own.shape[0]
    keys = 2 * half
    vmem = pl.BlockSpec(memory_space=pltpu.VMEM)
    flops = 2 * heads * count * keys * (3 * DK + 2 * DV)
    return pl.pallas_call(
        lambda *refs: grad_kernel(group, *refs),
        out_shape=(
            jax.ShapeDtypeStruct((heads, DK, count), jnp.bfloat16),
            jax.ShapeDtypeStruct((half, WIN + DV), jnp.float32),
            jax.ShapeDtypeStruct((half, WIN + DV), jnp.bfloat16),
        ),
        in_specs=[vmem] * 7,
        out_specs=(vmem, vmem, vmem),
        scratch_shapes=[
            pltpu.VMEM((keys, WIN), jnp.bfloat16),
            pltpu.VMEM((WIN, keys), jnp.bfloat16),
            pltpu.VMEM((keys, WIN), jnp.float32),
            pltpu.VMEM((keys, DV), jnp.float32),
        ],
        cost_estimate=pl.CostEstimate(flops=flops, bytes_accessed=8_000_000, transcendentals=heads * count * keys),
        compiler_params=pltpu.CompilerParams(vmem_limit_bytes=40 * 1024 * 1024),
        name=f"grads_{group}",
    )(q, do, own, par, lse, delta, mask)


def per_device(queries, comp_keys, comp_values, outputs, grad_out, log_sums, visible):
    pb = lax.axis_size("pb")
    ka = lax.axis_size("ka")
    chips = pb // 2
    core = lax.rem(lax.axis_index("pb"), 2)
    same_core = [[2 * i + c for i in range(chips)] for c in range(2)]
    other_core = [(i, i ^ 1) for i in range(pb)]
    rows = comp_keys.shape[0]
    groups = comp_keys.shape[1] // DK

    both = jnp.concatenate([comp_keys, comp_values], axis=1)
    own = lax.all_to_all(
        jnp.broadcast_to(both, (chips, *both.shape)), "pb", 0, 0, axis_index_groups=same_core, tiled=True
    ).reshape(chips * rows, both.shape[1])
    par = lax.ppermute(own, "pb", other_core)

    delta = [
        jnp.sum(
            grad_out[:, :, g * DV:(g + 1) * DV].astype(jnp.float32)
            * outputs[:, :, g * DV:(g + 1) * DV].astype(jnp.float32),
            axis=2,
        )
        for g in range(groups)
    ]
    seen = visible.reshape(visible.shape[0], chips, 2, rows)
    seen = jnp.where(core == 0, seen, seen[:, :, ::-1])
    seen = seen.transpose(2, 1, 3, 0).reshape(2 * chips * rows, visible.shape[0])
    mask = jnp.repeat(seen.astype(jnp.float32), QBLK, axis=1)

    heads, count, _ = queries.shape
    summed_q, summed_kv = [], []
    for g in range(groups):
        dqt, own_g, par_g = group_grads(g, queries, grad_out, own, par, log_sums[g], delta[g], mask)
        arrived = lax.all_to_all(dqt.reshape(ka, heads // ka, DK, count), "ka", 0, 0, tiled=True)
        summed_q.append(arrived)
        from_other = lax.ppermute(par_g, "pb", other_core)
        chip_sum = (own_g + from_other.astype(jnp.float32)).astype(jnp.bfloat16)
        pieces = lax.all_to_all(
            chip_sum.reshape(chips, rows, WIN + DV), "pb", 0, 0, axis_index_groups=same_core, tiled=True
        )
        summed_kv.append(pieces)
    dq = jnp.concatenate([a.astype(jnp.float32).sum(axis=0) for a in summed_q], axis=1).transpose(0, 2, 1)
    kv = [a.astype(jnp.float32).sum(axis=0) for a in summed_kv]
    dk = jnp.concatenate([kv[0][:, :DK], kv[1][:, WIN - DK:WIN]], axis=1)
    dv = jnp.concatenate([kv[0][:, WIN:], kv[1][:, WIN:]], axis=1)
    return (dq, dk, dv)


def solution(mesh):
    return jax.shard_map(
        per_device,
        mesh=mesh,
        in_specs=(
            P(None, "pb", "ga"),
            P(("ka", "pb"), "ga"),
            P(("ka", "pb"), "ga"),
            P(None, "pb", "ga"),
            P(None, "pb", "ga"),
            P("ga", None, "pb"),
            P("pb", "ka"),
        ),
        out_specs=(P("ka", "pb", "ga"), P(("ka", "pb"), "ga"), P(("ka", "pb"), "ga")),
        check_vma=False,
    )
```

```python
import math

import jax
import jax.numpy as jnp
from jax import lax
from jax.experimental import pallas as pl
from jax.experimental.pallas import tpu as pltpu
from jax.sharding import PartitionSpec as P

DK = 192
DV = 128
QBLK = 64
LANES = 128
GROUPS = 2
WIN = 256
SCALE = 1.0 / math.sqrt(DK)
LOG2E = math.log2(math.e)
KEY_TILE = 256
HEADS = 4
NT = (((1,), (1,)), ((), ()))
NN = (((1,), (0,)), ((), ()))


def dot(a, b, dims):
    return lax.dot_general(a, b, dims, preferred_element_type=jnp.float32)


def key_tiles(own_ref, par_ref):
    half = own_ref.shape[0]
    return [
        (ref, t * KEY_TILE, side * half + t * KEY_TILE)
        for side, ref in enumerate((own_ref, par_ref))
        for t in range(half // KEY_TILE)
    ]


def key_window(group, ref, at):
    lane = lax.broadcasted_iota(jnp.int32, (KEY_TILE, WIN), 1)
    keep = (lane < DK) if group == 0 else (lane >= WIN - DK)
    lo = group * LANES
    return jnp.where(keep, ref[at:at + KEY_TILE, lo:lo + WIN], jnp.zeros((), jnp.bfloat16))


def chunk_rows(group, h, q_ref, do_ref, lse_ref, delta_ref):
    rows = HEADS * q_ref.shape[1]
    lo = group * LANES
    q = q_ref[pl.ds(h, HEADS), :, lo:lo + WIN].reshape(rows, WIN)
    do = do_ref[pl.ds(h, HEADS), :, lo:lo + DV].reshape(rows, DV)
    lse = jnp.concatenate([lse_ref[group, pl.ds(h + j, 1), :] for j in range(HEADS)], axis=1) * LOG2E
    delta = jnp.concatenate([delta_ref[group, pl.ds(h + j, 1), :] for j in range(HEADS)], axis=1)
    return q, do, lse, delta


def tile_terms(key, value, mask, q, do, lse, delta):
    s = dot(key, q, NT)
    dp = dot(value, do, NT)
    p = jnp.exp2(s * (SCALE * LOG2E) - lse) * jnp.concatenate([mask] * HEADS, axis=1)
    ds = (p * (dp - delta)).astype(jnp.bfloat16)
    return p.astype(jnp.bfloat16), ds


def query_kernel(q_ref, do_ref, own_ref, par_ref, lse_ref, delta_ref, mask_ref, dqt_ref, kz, kt):
    tiles = key_tiles(own_ref, par_ref)
    for group in range(GROUPS):
        vlo = 3 * LANES + group * LANES
        first = 0 if group == 0 else WIN - DK
        for ref, at, row in tiles:
            k = key_window(group, ref, at)
            kz[row:row + KEY_TILE, :] = k
            kt[:, row:row + KEY_TILE] = k.T

        def chunk(i, carry):
            h = i * HEADS
            q, do, lse, delta = chunk_rows(group, h, q_ref, do_ref, lse_ref, delta_ref)
            dqt = jnp.zeros((DK, q.shape[0]), jnp.float32)
            for ref, at, row in tiles:
                _, ds = tile_terms(
                    kz[row:row + KEY_TILE, :], ref[at:at + KEY_TILE, vlo:vlo + DV],
                    mask_ref[row:row + KEY_TILE, :], q, do, lse, delta,
                )
                dqt = dqt + dot(kt[first:first + DK, row:row + KEY_TILE], ds, NN)
            dqt = (dqt * SCALE).astype(jnp.bfloat16)
            for j in range(HEADS):
                dqt_ref[h + j, group * DK:(group + 1) * DK, :] = dqt[:, j * LANES:(j + 1) * LANES]
            return carry

        lax.fori_loop(0, q_ref.shape[0] // HEADS, chunk, 0)


def key_kernel(q_ref, do_ref, own_ref, par_ref, lse_ref, delta_ref, mask_ref, own_out, par_out, kz, acc_k, acc_v):
    half = own_ref.shape[0]
    tiles = key_tiles(own_ref, par_ref)
    for group in range(GROUPS):
        vlo = 3 * LANES + group * LANES
        for ref, at, row in tiles:
            kz[row:row + KEY_TILE, :] = key_window(group, ref, at)
        acc_k[group, :, :] = jnp.zeros(acc_k.shape[1:], jnp.float32)
        acc_v[...] = jnp.zeros_like(acc_v)

        def chunk(i, carry):
            q, do, lse, delta = chunk_rows(group, i * HEADS, q_ref, do_ref, lse_ref, delta_ref)
            for ref, at, row in tiles:
                p, ds = tile_terms(
                    kz[row:row + KEY_TILE, :], ref[at:at + KEY_TILE, vlo:vlo + DV],
                    mask_ref[row:row + KEY_TILE, :], q, do, lse, delta,
                )
                acc_v[row:row + KEY_TILE, :] += dot(p, do, NN)
                acc_k[group, row:row + KEY_TILE, :] += dot(ds, q, NN)
            return carry

        lax.fori_loop(0, q_ref.shape[0] // HEADS, chunk, 0)
        own_out[:, vlo:vlo + DV] = acc_v[:half, :]
        par_out[:, vlo:vlo + DV] = acc_v[half:, :].astype(par_out.dtype)
    low = lax.broadcasted_iota(jnp.int32, (half, LANES), 1) < DK - LANES
    for side, out in enumerate((own_out, par_out)):
        at = side * half
        a = acc_k[0, at:at + half, :] * SCALE
        b = acc_k[1, at:at + half, :] * SCALE
        out[:, :LANES] = a[:, :LANES].astype(out.dtype)
        out[:, LANES:2 * LANES] = jnp.where(low, a[:, LANES:], b[:, :LANES]).astype(out.dtype)
        out[:, 2 * LANES:3 * LANES] = b[:, LANES:].astype(out.dtype)


def grads(q, do, own, par, lse, delta, mask, which):
    heads, count, width = q.shape
    half, both = own.shape
    keys = 2 * half
    vmem = pl.BlockSpec(memory_space=pltpu.VMEM)
    work = 2 * GROUPS * heads * count * keys
    if which == "query":
        return pl.pallas_call(
            query_kernel,
            out_shape=jax.ShapeDtypeStruct((heads, width, count), jnp.bfloat16),
            in_specs=[vmem] * 7,
            out_specs=vmem,
            scratch_shapes=[pltpu.VMEM((keys, WIN), jnp.bfloat16), pltpu.VMEM((WIN, keys), jnp.bfloat16)],
            cost_estimate=pl.CostEstimate(
                flops=work * (2 * DK + DV), bytes_accessed=7_000_000, transcendentals=work // 2),
            compiler_params=pltpu.CompilerParams(vmem_limit_bytes=24 * 1024 * 1024),
            name="query_grads",
        )(q, do, own, par, lse, delta, mask)
    return pl.pallas_call(
        key_kernel,
        out_shape=(
            jax.ShapeDtypeStruct((half, both), jnp.float32),
            jax.ShapeDtypeStruct((half, both), jnp.bfloat16),
        ),
        in_specs=[vmem] * 7,
        out_specs=(vmem, vmem),
        scratch_shapes=[
            pltpu.VMEM((keys, WIN), jnp.bfloat16),
            pltpu.VMEM((GROUPS, keys, WIN), jnp.float32),
            pltpu.VMEM((keys, DV), jnp.float32),
        ],
        cost_estimate=pl.CostEstimate(
            flops=work * 2 * (DK + DV), bytes_accessed=8_000_000, transcendentals=work // 2),
        compiler_params=pltpu.CompilerParams(vmem_limit_bytes=24 * 1024 * 1024),
        name="key_grads",
    )(q, do, own, par, lse, delta, mask)


def per_device(queries, comp_keys, comp_values, outputs, grad_out, log_sums, visible):
    pb = lax.axis_size("pb")
    ka = lax.axis_size("ka")
    chips = pb // 2
    core = lax.rem(lax.axis_index("pb"), 2)
    same_core = [[2 * i + c for i in range(chips)] for c in range(2)]
    other_core = [(i, i ^ 1) for i in range(pb)]
    rows = comp_keys.shape[0]
    heads, count, width = queries.shape

    both = jnp.concatenate([comp_keys, comp_values], axis=1)
    own = lax.all_to_all(
        jnp.broadcast_to(both, (chips, *both.shape)), "pb", 0, 0, axis_index_groups=same_core, tiled=True
    ).reshape(chips * rows, both.shape[1])
    delta = jnp.stack([
        jnp.sum(
            grad_out[:, :, g * DV:(g + 1) * DV].astype(jnp.float32)
            * outputs[:, :, g * DV:(g + 1) * DV].astype(jnp.float32),
            axis=2,
        )
        for g in range(GROUPS)
    ])
    seen = visible.reshape(visible.shape[0], chips, 2, rows)
    seen = jnp.where(core == 0, seen, seen[:, :, ::-1])
    seen = seen.transpose(2, 1, 3, 0).reshape(2 * chips * rows, visible.shape[0])
    mask = jnp.repeat(seen.astype(jnp.float32), QBLK, axis=1)
    own, delta, mask = lax.optimization_barrier((own, delta, mask))
    par = lax.ppermute(own, "pb", other_core)

    args = (queries, grad_out, own, par, log_sums, delta, mask)
    dqt = grads(*args, "query")
    arrived_q = lax.all_to_all(dqt.reshape(ka, heads // ka, width, count), "ka", 0, 0, tiled=True)

    own_kv, par_kv = grads(*args, "key")
    from_other = lax.ppermute(par_kv, "pb", other_core)
    chip_sum = (own_kv + from_other.astype(jnp.float32)).astype(jnp.bfloat16)
    arrived_kv = lax.all_to_all(
        chip_sum.reshape(chips, rows, both.shape[1]), "pb", 0, 0, axis_index_groups=same_core, tiled=True
    )
    kv = arrived_kv.astype(jnp.float32).sum(axis=0)
    dq = arrived_q.astype(jnp.float32).sum(axis=0).transpose(0, 2, 1)
    return (dq, kv[:, :width], kv[:, width:])


def solution(mesh):
    return jax.shard_map(
        per_device,
        mesh=mesh,
        in_specs=(
            P(None, "pb", "ga"),
            P(("ka", "pb"), "ga"),
            P(("ka", "pb"), "ga"),
            P(None, "pb", "ga"),
            P(None, "pb", "ga"),
            P("ga", None, "pb"),
            P("pb", "ka"),
        ),
        out_specs=(P("ka", "pb", "ga"), P(("ka", "pb"), "ga"), P(("ka", "pb"), "ga")),
        check_vma=False,
    )
```

```python
import math

import jax
import jax.numpy as jnp
from jax import lax
from jax.experimental import pallas as pl
from jax.experimental.pallas import tpu as pltpu
from jax.sharding import PartitionSpec as P

DK = 192
DV = 128
QBLK = 64
LANES = 128
GROUPS = 2
WIN = 256
SCALE = 1.0 / math.sqrt(DK)
LOG2E = math.log2(math.e)
KEY_TILE = 256
FAR = (3, -3, 4)
NEAR = (0, 1, -1, 2, -2)
NT = (((1,), (1,)), ((), ()))
NN = (((1,), (0,)), ((), ()))


def dot(a, b, dims):
    return lax.dot_general(a, b, dims, preferred_element_type=jnp.float32)


def key_tiles(own_ref, par_ref):
    half = own_ref.shape[0]
    return [
        (ref, t * KEY_TILE, side * half + t * KEY_TILE)
        for side, ref in enumerate((own_ref, par_ref))
        for t in range(half // KEY_TILE)
    ]


def load_keys(own_ref, par_ref, kz, kt):
    lane = lax.broadcasted_iota(jnp.int32, (KEY_TILE, WIN), 1)
    for group in range(GROUPS):
        keep = (lane < DK) if group == 0 else (lane >= WIN - DK)
        lo = group * LANES
        first = 0 if group == 0 else WIN - DK
        for ref, at, row in key_tiles(own_ref, par_ref):
            k = jnp.where(keep, ref[at:at + KEY_TILE, lo:lo + WIN], jnp.zeros((), jnp.bfloat16))
            kz[group, row:row + KEY_TILE, :] = k
            kt[group, :, row:row + KEY_TILE] = k.T[first:first + DK, :]


def owner_grads(h, per_owner, q_ref, do_ref, own_ref, par_ref, lse_ref, delta_ref, mask_ref, kz, kt, acc_k, acc_v):
    rows = per_owner * q_ref.shape[1]
    result = []
    for group in range(GROUPS):
        lo = group * LANES
        vlo = 3 * LANES + lo
        q = q_ref[pl.ds(h, per_owner), :, lo:lo + WIN].reshape(rows, WIN)
        do = do_ref[pl.ds(h, per_owner), :, lo:lo + DV].reshape(rows, DV)
        lse = jnp.concatenate([lse_ref[group, pl.ds(h + j, 1), :] for j in range(per_owner)], axis=1) * LOG2E
        delta = jnp.concatenate([delta_ref[group, pl.ds(h + j, 1), :] for j in range(per_owner)], axis=1)
        dqt = jnp.zeros((DK, rows), jnp.float32)
        for ref, at, row in key_tiles(own_ref, par_ref):
            s = dot(kz[group, row:row + KEY_TILE, :], q, NT)
            dp = dot(ref[at:at + KEY_TILE, vlo:vlo + DV], do, NT)
            mask = jnp.concatenate([mask_ref[row:row + KEY_TILE, :]] * per_owner, axis=1)
            p = jnp.exp2(s * (SCALE * LOG2E) - lse) * mask
            ds = (p * (dp - delta)).astype(jnp.bfloat16)
            acc_v[group, row:row + KEY_TILE, :] += dot(p.astype(jnp.bfloat16), do, NN)
            acc_k[group, row:row + KEY_TILE, :] += dot(ds, q, NN)
            dqt = dqt + dot(kt[group, :, row:row + KEY_TILE], ds, NN)
        result.append(dqt * SCALE)
    return result


def far_kernel(heads_ref, *refs):
    inputs, (right, left, acc_k, acc_v), (kz, kt, held) = refs[:7], refs[7:11], refs[11:]
    per_owner = right.shape[0]
    load_keys(inputs[2], inputs[3], kz, kt)
    acc_k[...] = jnp.zeros_like(acc_k)
    acc_v[...] = jnp.zeros_like(acc_v)

    def one(i, carry):
        dqt = owner_grads(heads_ref[i], per_owner, *inputs, kz, kt, acc_k, acc_v)
        for group in range(GROUPS):
            for j in range(per_owner):
                held[i, j, group * DK:(group + 1) * DK, :] = dqt[group][:, j * LANES:(j + 1) * LANES].astype(held.dtype)
        return carry

    lax.fori_loop(0, len(FAR), one, 0)
    width = GROUPS * DK
    right[:, :width, :] = held[0]
    left[:, :width, :] = held[1]
    right[:, width:, :] = held[2, :, :DK, :]
    left[:, width:, :] = held[2, :, DK:, :]


def near_kernel(heads_ref, *refs):
    inputs, (in_k, in_v), (near, own_out, par_out), (kz, kt, acc_k, acc_v) = refs[:7], refs[7:9], refs[9:12], refs[12:]
    per_owner = near.shape[1]
    half = own_out.shape[0]
    load_keys(inputs[2], inputs[3], kz, kt)
    acc_k[...] = in_k[...]
    acc_v[...] = in_v[...]

    def one(i, carry):
        dqt = owner_grads(heads_ref[len(FAR) + i], per_owner, *inputs, kz, kt, acc_k, acc_v)
        for group in range(GROUPS):
            for j in range(per_owner):
                near[i, j, group * DK:(group + 1) * DK, :] = dqt[group][:, j * LANES:(j + 1) * LANES]
        return carry

    lax.fori_loop(0, len(NEAR), one, 0)
    low = lax.broadcasted_iota(jnp.int32, (half, LANES), 1) < DK - LANES
    for side, out in enumerate((own_out, par_out)):
        at = side * half
        a = acc_k[0, at:at + half, :] * SCALE
        b = acc_k[1, at:at + half, :] * SCALE
        out[:, :LANES] = a[:, :LANES].astype(out.dtype)
        out[:, LANES:2 * LANES] = jnp.where(low, a[:, LANES:], b[:, :LANES]).astype(out.dtype)
        out[:, 2 * LANES:3 * LANES] = b[:, LANES:].astype(out.dtype)
        for group in range(GROUPS):
            vlo = (3 + group) * LANES
            out[:, vlo:vlo + DV] = acc_v[group, at:at + half, :].astype(out.dtype)


def call(kernel, name, owners, per_owner, outs, scratch, *args):
    half = args[3].shape[0]
    count = args[1].shape[1]
    work = 2 * GROUPS * owners * per_owner * count * 2 * half
    vmem = pl.BlockSpec(memory_space=pltpu.VMEM)
    return pl.pallas_call(
        kernel,
        out_shape=outs,
        in_specs=[pl.BlockSpec(memory_space=pltpu.SMEM)] + [vmem] * (len(args) - 1),
        out_specs=tuple(vmem for _ in outs),
        scratch_shapes=[
            pltpu.VMEM((GROUPS, 2 * half, WIN), jnp.bfloat16),
            pltpu.VMEM((GROUPS, DK, 2 * half), jnp.bfloat16),
            *scratch,
        ],
        cost_estimate=pl.CostEstimate(
            flops=work * (3 * DK + 2 * DV), bytes_accessed=10_000_000, transcendentals=work // 2),
        compiler_params=pltpu.CompilerParams(vmem_limit_bytes=24 * 1024 * 1024),
        name=name,
    )(*args)


def per_device(queries, comp_keys, comp_values, outputs, grad_out, log_sums, visible):
    pb = lax.axis_size("pb")
    ka = lax.axis_size("ka")
    chips = pb // 2
    core = lax.rem(lax.axis_index("pb"), 2)
    me = lax.axis_index("ka")
    same_core = [[2 * i + c for i in range(chips)] for c in range(2)]
    other_core = [(i, i ^ 1) for i in range(pb)]
    rows = comp_keys.shape[0]
    heads, count, width = queries.shape
    per_owner = heads // ka
    f32, bf16 = jnp.float32, jnp.bfloat16

    def along(x, step):
        return lax.ppermute(x, "ka", [(i, (i + step) % ka) for i in range(ka)])

    both = jnp.concatenate([comp_keys, comp_values], axis=1)
    keys = 2 * chips * rows
    half = keys // 2
    own = lax.all_to_all(
        jnp.broadcast_to(both, (chips, *both.shape)), "pb", 0, 0, axis_index_groups=same_core, tiled=True
    ).reshape(half, both.shape[1])
    delta = jnp.stack([
        jnp.sum(
            grad_out[:, :, g * DV:(g + 1) * DV].astype(f32) * outputs[:, :, g * DV:(g + 1) * DV].astype(f32), axis=2
        )
        for g in range(GROUPS)
    ])
    seen = visible.reshape(visible.shape[0], chips, 2, rows)
    seen = jnp.where(core == 0, seen, seen[:, :, ::-1])
    seen = seen.transpose(2, 1, 3, 0).reshape(keys, visible.shape[0])
    mask = jnp.repeat(seen.astype(f32), QBLK, axis=1)
    order = per_owner * ((me + jnp.array(FAR + NEAR, jnp.int32) + ka) % ka)
    own, delta, mask, order = lax.optimization_barrier((own, delta, mask, order))
    par = lax.ppermute(own, "pb", other_core)

    args = (order, queries, grad_out, own, par, log_sums, delta, mask)
    shape = jax.ShapeDtypeStruct
    hops = shape((per_owner, width + DK, count), bf16)
    right, left, acc_k, acc_v = call(
        far_kernel, "far_grads", len(FAR), per_owner,
        (hops, hops, shape((GROUPS, keys, WIN), f32), shape((GROUPS, keys, DV), f32)),
        [pltpu.VMEM((len(FAR), per_owner, width, count), bf16)], *args,
    )
    with jax.named_scope("step1"):
        from_left = along(right, 2)
        from_right = along(left, -2)
    near, own_kv, par_kv = call(
        near_kernel, "near_grads", len(NEAR), per_owner,
        (
            shape((len(NEAR), per_owner, width, count), f32),
            shape((half, both.shape[1]), f32),
            shape((half, both.shape[1]), bf16),
        ),
        [pltpu.VMEM((GROUPS, keys, WIN), f32), pltpu.VMEM((GROUPS, keys, DV), f32)], *args, acc_k, acc_v,
    )
    from_other = lax.ppermute(par_kv, "pb", other_core)

    from_left, from_right = from_left.astype(f32), from_right.astype(f32)
    up1 = near[1] + from_left[:, :width]
    down1 = near[2] + from_right[:, :width]
    up2 = jnp.concatenate([near[3, :, :DK] + from_left[:, width:], near[3, :, DK:]], axis=1)
    down2 = jnp.concatenate([near[4, :, :DK], near[4, :, DK:] + from_right[:, width:]], axis=1)
    with jax.named_scope("step2"):
        arrived = [
            along(x.astype(bf16), step) for x, step in ((up2, 2), (down2, -2), (up1, 1), (down1, -1))
        ]
    chip_sum = (own_kv + from_other.astype(f32)).astype(bf16)
    arrived_kv = lax.all_to_all(
        chip_sum.reshape(chips, rows, both.shape[1]), "pb", 0, 0, axis_index_groups=same_core, tiled=True
    )
    kv = arrived_kv.astype(f32).sum(axis=0)
    dq = near[0] + sum(x.astype(f32) for x in arrived)
    return (dq.transpose(0, 2, 1), kv[:, :width], kv[:, width:])


def solution(mesh):
    return jax.shard_map(
        per_device,
        mesh=mesh,
        in_specs=(
            P(None, "pb", "ga"),
            P(("ka", "pb"), "ga"),
            P(("ka", "pb"), "ga"),
            P(None, "pb", "ga"),
            P(None, "pb", "ga"),
            P("ga", None, "pb"),
            P("pb", "ka"),
        ),
        out_specs=(P("ka", "pb", "ga"), P(("ka", "pb"), "ga"), P(("ka", "pb"), "ga")),
        check_vma=False,
    )
```

```python
import math

import jax
import jax.numpy as jnp
from jax import lax
from jax.experimental import pallas as pl
from jax.experimental.pallas import tpu as pltpu
from jax.sharding import PartitionSpec as P


DK = 192
DV = 128
QBLK = 64
LANES = 128
GROUPS = 2
WIN = 256
SCALE = 1.0 / math.sqrt(DK)
LOG2E = math.log2(math.e)
FAR = (3, 5, 4)
NEAR = (0, 1, 7, 2, 6)
KA = 8
GRANT = 67_000_000
NT = (((1,), (1,)), ((), ()))
NN = (((1,), (0,)), ((), ()))
VMEM = pl.BlockSpec(memory_space=pltpu.VMEM)
HBM = pl.BlockSpec(memory_space=pltpu.HBM)


def dot(a, b, dims):
    return lax.dot_general(a, b, dims, preferred_element_type=jnp.float32)


def pick(i, values):
    result = jnp.int32(values[0])
    for n, value in enumerate(values[1:], 1):
        result = jnp.where(i == n, jnp.int32(value), result)
    return result


def load_keys(copies, kv_buf, kz, vz, kt):
    half = kv_buf.shape[1]
    lane = lax.broadcasted_iota(jnp.int32, (half, WIN), 1)
    for side, copy in enumerate(copies):
        copy.wait()
        at = side * half
        for group in range(GROUPS):
            keep = (lane < DK) if group == 0 else (lane >= WIN - DK)
            lo = group * LANES
            vlo = 3 * LANES + lo
            first = 0 if group == 0 else WIN - DK
            k = jnp.where(keep, kv_buf[side, :, lo:lo + WIN], jnp.zeros((), jnp.bfloat16))
            kz[group, at:at + half, :] = k
            vz[group, at:at + half, :] = kv_buf[side, :, vlo:vlo + DV]
            kt[group, :, at:at + half] = k.T[first:first + DK, :]


def start_copies(owners, h_of, q_hbm, do_hbm, own_hbm, par_hbm, mask_hbm, q_buf, do_buf, kv_buf, mask_buf, sems, others):
    per_owner = q_buf.shape[1]
    keys = [
        pltpu.make_async_copy(own_hbm, kv_buf.at[0], others.at[0]),
        pltpu.make_async_copy(par_hbm, kv_buf.at[1], others.at[1]),
    ]
    mask = pltpu.make_async_copy(mask_hbm, mask_buf, others.at[2])
    for copy in keys:
        copy.start()

    def copies(i, h):
        return (
            pltpu.make_async_copy(q_hbm.at[pl.ds(h, per_owner)], q_buf.at[i], sems.at[0, i]),
            pltpu.make_async_copy(do_hbm.at[pl.ds(h, per_owner)], do_buf.at[i], sems.at[1, i]),
        )

    for i in range(owners):
        for copy in copies(i, h_of(i)):
            copy.start()
        if i == 0:
            mask.start()
    return keys, mask, copies


def group_terms(group, i, h, q_buf, do_buf, lse_ref, delta_ref, mask_ref, kz, vz):
    per_owner, count = q_buf.shape[1:3]
    rows = per_owner * count
    lo = group * LANES
    q = q_buf[i, :, :, lo:lo + WIN].reshape(rows, WIN)
    do = do_buf[i, :, :, lo:lo + DV].reshape(rows, DV)
    lse = jnp.concatenate([lse_ref[group, pl.ds(h + j, 1), :] for j in range(per_owner)], axis=1) * LOG2E
    delta = jnp.concatenate([delta_ref[group, pl.ds(h + j, 1), :] for j in range(per_owner)], axis=1)
    s = dot(kz[group], q, NT)
    dp = dot(vz[group], do, NT)
    p = jnp.exp2(s * (SCALE * LOG2E) - lse) * jnp.concatenate([mask_ref[...]] * per_owner, axis=1)
    ds = (p * (dp - delta)).astype(jnp.bfloat16)
    return q, do, p.astype(jnp.bfloat16), ds


def far_kernel(q_hbm, do_hbm, own_hbm, par_hbm, mask_hbm, lse_ref, delta_ref, right, left,
               q_buf, do_buf, kv_buf, mask_ref, kz, vz, kt, held, sems, others):
    per_owner, _, count = right.shape
    me = lax.axis_index("ka")
    h_of = lambda i: per_owner * lax.rem(me + pick(i, FAR), KA)
    key_copies, mask_copy, copies = start_copies(
        len(FAR), h_of, q_hbm, do_hbm, own_hbm, par_hbm, mask_hbm, q_buf, do_buf, kv_buf, mask_ref, sems, others)
    load_keys(key_copies, kv_buf, kz, vz, kt)
    mask_copy.wait()

    def one(i, carry):
        h = h_of(i)
        for copy in copies(i, h):
            copy.wait()
        for group in range(GROUPS):
            _, _, _, ds = group_terms(group, i, h, q_buf, do_buf, lse_ref, delta_ref, mask_ref, kz, vz)
            dqt = dot(kt[group], ds, NN) * SCALE
            for j in range(per_owner):
                held[i, j, group * DK:(group + 1) * DK, :] = dqt[:, j * count:(j + 1) * count].astype(held.dtype)
        return carry

    lax.fori_loop(0, len(FAR), one, 0)
    width = GROUPS * DK
    right[:, :width, :] = held[0]
    left[:, :width, :] = held[1]
    right[:, width:, :] = held[2, :, :DK, :]
    left[:, width:, :] = held[2, :, DK:, :]


def near_kernel(q_hbm, do_hbm, own_hbm, par_hbm, mask_hbm, lse_ref, delta_ref, after, home, near, own_out, par_out,
                q_buf, do_buf, kv_buf, mask_ref, kz, vz, kt, acc_k, acc_v, near_buf, sems, others):
    del after
    per_owner, _, count = home.shape
    half = own_out.shape[0]
    me = lax.axis_index("ka")
    steps = NEAR + FAR
    h_of = lambda i: per_owner * lax.rem(me + pick(i, steps), KA)
    key_copies, mask_copy, copies = start_copies(
        KA, h_of, q_hbm, do_hbm, own_hbm, par_hbm, mask_hbm, q_buf, do_buf, kv_buf, mask_ref, sems, others)
    load_keys(key_copies, kv_buf, kz, vz, kt)
    mask_copy.wait()
    acc_k[...] = jnp.zeros_like(acc_k)
    acc_v[...] = jnp.zeros_like(acc_v)

    def one(i, query_grads):
        h = h_of(i)
        for copy in copies(i, h):
            copy.wait()
        for group in range(GROUPS):
            q, do, p, ds = group_terms(group, i, h, q_buf, do_buf, lse_ref, delta_ref, mask_ref, kz, vz)
            acc_v[group] += dot(p, do, NN)
            acc_k[group] += dot(ds, q, NN)
            if query_grads is not None:
                dqt = dot(kt[group], ds, NN) * SCALE
                for j in range(per_owner):
                    query_grads(j, slice(group * DK, (group + 1) * DK), dqt[:, j * count:(j + 1) * count])


    def near_one(i, carry):
        def to_near(j, where, value):
            near_buf[i, j, where, :] = value

        one(i, to_near)
        return carry

    def far_one(i, carry):
        one(i, None)
        return carry

    lax.fori_loop(0, len(NEAR), near_one, 0)
    results = (
        pltpu.make_async_copy(near_buf.at[0], home, others.at[0]),
        pltpu.make_async_copy(near_buf.at[pl.ds(1, len(NEAR) - 1)], near, others.at[1]),
    )
    for copy in results:
        copy.start()
    lax.fori_loop(len(NEAR), KA, far_one, 0)
    low = lax.broadcasted_iota(jnp.int32, (half, LANES), 1) < DK - LANES
    for side, out in enumerate((own_out, par_out)):
        at = side * half
        a = acc_k[0, at:at + half, :] * SCALE
        b = acc_k[1, at:at + half, :] * SCALE
        out[:, :LANES] = a[:, :LANES].astype(out.dtype)
        out[:, LANES:2 * LANES] = jnp.where(low, a[:, LANES:], b[:, :LANES]).astype(out.dtype)
        out[:, 2 * LANES:3 * LANES] = b[:, LANES:].astype(out.dtype)
        for group in range(GROUPS):
            vlo = (3 + group) * LANES
            out[:, vlo:vlo + DV] = acc_v[group, at:at + half, :].astype(out.dtype)
    for copy in results:
        copy.wait()


def grads(kernel, owners, matmuls, outs, out_specs, scratch, q, do, own, par, mask, lse, delta, *after):
    heads, count, width = q.shape
    per_owner = heads // KA
    keys = 2 * own.shape[0]
    bf16 = jnp.bfloat16
    return pl.pallas_call(
        kernel,
        out_shape=outs,
        in_specs=[HBM] * 5 + [VMEM] * 2 + [HBM] * len(after),
        out_specs=out_specs,
        scratch_shapes=[
            pltpu.VMEM((owners, per_owner, count, width), bf16),
            pltpu.VMEM((owners, per_owner, count, do.shape[2]), bf16),
            pltpu.VMEM((2, *own.shape), bf16),
            pltpu.VMEM(mask.shape, mask.dtype),
            pltpu.VMEM((GROUPS, keys, WIN), bf16),
            pltpu.VMEM((GROUPS, keys, DV), bf16),
            pltpu.VMEM((GROUPS, DK, keys), bf16),
            *scratch,
            pltpu.SemaphoreType.DMA((2, owners)),
            pltpu.SemaphoreType.DMA((3,)),
        ],
        cost_estimate=pl.CostEstimate(
            flops=2 * GROUPS * owners * per_owner * count * keys * matmuls, bytes_accessed=6_000_000,
            transcendentals=GROUPS * owners * per_owner * count * keys),
        compiler_params=pltpu.CompilerParams(vmem_limit_bytes=GRANT),
    )(q, do, own, par, mask, lse, delta, *after)


def small(kernel, outs, *args, out_specs=None):
    return pl.pallas_call(
        kernel,
        out_shape=outs,
        in_specs=[VMEM] * len(args),
        out_specs=out_specs or tuple(VMEM for _ in outs),
        compiler_params=pltpu.CompilerParams(vmem_limit_bytes=16 * 1024 * 1024),
    )(*args)


def copies_kernel(keys, values, out):
    width = keys.shape[1]
    for i in range(out.shape[0]):
        out[i, :, :width] = keys[...]
        out[i, :, width:] = values[...]


def message_kernel(near, from_left, from_right, up2, down2, up1, down1):
    f32, bf16 = jnp.float32, jnp.bfloat16
    width = up1.shape[1]
    up1[...] = (near[0] + from_left[:, :width, :].astype(f32)).astype(bf16)
    down1[...] = (near[1] + from_right[:, :width, :].astype(f32)).astype(bf16)
    up2[:, :DK, :] = (near[2, :, :DK, :] + from_left[:, width:, :].astype(f32)).astype(bf16)
    up2[:, DK:, :] = near[2, :, DK:, :].astype(bf16)
    down2[:, :DK, :] = near[3, :, :DK, :].astype(bf16)
    down2[:, DK:, :] = (near[3, :, DK:, :] + from_right[:, width:, :].astype(f32)).astype(bf16)


def finish_kernel(home, a, b, c, d, pieces, dq, dk, dv):
    f32 = jnp.float32
    for j in range(home.shape[0]):
        total = home[j] + ((a[j].astype(f32) + b[j].astype(f32)) + (c[j].astype(f32) + d[j].astype(f32)))
        dq[j] = total.T
    kv = pieces[0].astype(f32)
    for i in range(1, pieces.shape[0]):
        kv = kv + pieces[i].astype(f32)
    width = dk.shape[1]
    dk[...] = kv[:, :width]
    dv[...] = kv[:, width:]


def per_device(queries, comp_keys, comp_values, outputs, grad_out, log_sums, visible):
    pb = lax.axis_size("pb")
    ka = lax.axis_size("ka")
    chips = pb // 2
    core = lax.rem(lax.axis_index("pb"), 2)
    same_core = [[2 * i + c for i in range(chips)] for c in range(2)]
    other_core = [(i, i ^ 1) for i in range(pb)]
    rows, width = comp_keys.shape
    both = width + comp_values.shape[1]
    heads, count, _ = queries.shape
    per_owner = heads // ka
    keys = 2 * chips * rows
    half = keys // 2
    f32, bf16 = jnp.float32, jnp.bfloat16
    shape = jax.ShapeDtypeStruct

    def along(x, step):
        return lax.ppermute(x, "ka", [(i, (i + step) % ka) for i in range(ka)])

    (copies,) = small(copies_kernel, (shape((chips, rows, both), bf16),), comp_keys, comp_values)
    own = lax.all_to_all(copies, "pb", 0, 0, axis_index_groups=same_core, tiled=True).reshape(half, both)
    delta = jnp.stack([
        jnp.sum(
            grad_out[:, :, g * DV:(g + 1) * DV].astype(f32) * outputs[:, :, g * DV:(g + 1) * DV].astype(f32), axis=2
        )
        for g in range(GROUPS)
    ])
    seen = visible.reshape(visible.shape[0], chips, 2, rows)
    seen = jnp.where(core == 0, seen, seen[:, :, ::-1])
    seen = seen.transpose(2, 1, 3, 0).reshape(keys, visible.shape[0])
    mask = jnp.repeat(seen.astype(f32), QBLK, axis=1)
    own, delta, mask = lax.optimization_barrier((own, delta, mask))
    par = lax.ppermute(own, "pb", other_core)

    args = (queries, grad_out, own, par, mask, log_sums, delta)
    hops = shape((per_owner, width + DK, count), bf16)
    chunk = (per_owner, width, count)
    right, left = grads(
        far_kernel, len(FAR), 2 * DK + DV, (hops, hops), (VMEM, VMEM), [pltpu.VMEM((len(FAR), *chunk), bf16)], *args
    )
    from_left = along(right, 2)
    from_right = along(left, -2)
    home, near, own_kv, par_kv = grads(
        near_kernel, KA, 3 * DK + 2 * DV,
        (shape(chunk, f32), shape((len(NEAR) - 1, *chunk), f32), shape((half, both), f32), shape((half, both), bf16)),
        (HBM, HBM, VMEM, VMEM),
        [
            pltpu.VMEM((GROUPS, keys, WIN), f32),
            pltpu.VMEM((GROUPS, keys, DV), f32),
            pltpu.VMEM((len(NEAR), *chunk), f32),
        ],
        *args, right,
    )
    from_other = lax.ppermute(par_kv, "pb", other_core)

    messages = small(message_kernel, (shape(chunk, bf16),) * 4, near, from_left, from_right)
    arrived = [along(x, step) for x, step in zip(messages, (2, -2, 1, -1))]
    chip_sum = (own_kv + from_other.astype(f32)).astype(bf16)
    pieces = lax.all_to_all(
        chip_sum.reshape(chips, rows, both), "pb", 0, 0, axis_index_groups=same_core, tiled=True
    )
    return small(
        finish_kernel,
        (shape((per_owner, count, width), f32), shape((rows, width), f32), shape((rows, both - width), f32)),
        home, *arrived, pieces,
    )


def solution(mesh):
    return jax.shard_map(
        per_device,
        mesh=mesh,
        in_specs=(
            P(None, "pb", "ga"),
            P(("ka", "pb"), "ga"),
            P(("ka", "pb"), "ga"),
            P(None, "pb", "ga"),
            P(None, "pb", "ga"),
            P("ga", None, "pb"),
            P("pb", "ka"),
        ),
        out_specs=(P("ka", "pb", "ga"), P(("ka", "pb"), "ga"), P(("ka", "pb"), "ga")),
        check_vma=False,
    )
```

```python
import math

import jax
import jax.numpy as jnp
from jax import lax
from jax.experimental import pallas as pl
from jax.experimental.pallas import tpu as pltpu
from jax.sharding import PartitionSpec as P


DK = 192
DV = 128
QBLK = 64
LANES = 128
GROUPS = 2
WIN = 256
SCALE = 1.0 / math.sqrt(DK)
LOG2E = math.log2(math.e)
FAR = (3, 5, 4)
NEAR = (0, 1, 7, 2, 6)
KA = 8
GRANT = 67_000_000
NT = (((1,), (1,)), ((), ()))
NN = (((1,), (0,)), ((), ()))
VMEM = pl.BlockSpec(memory_space=pltpu.VMEM)
HBM = pl.BlockSpec(memory_space=pltpu.HBM)


def dot(a, b, dims):
    return lax.dot_general(a, b, dims, preferred_element_type=jnp.float32)


def pick(i, values):
    result = jnp.int32(values[0])
    for n, value in enumerate(values[1:], 1):
        result = jnp.where(i == n, jnp.int32(value), result)
    return result


def load_keys(copies, kv_buf, kz, kt):
    half = kv_buf.shape[0] // 2
    lane = lax.broadcasted_iota(jnp.int32, (half, WIN), 1)
    one = lax.broadcasted_iota(jnp.int32, (DK, WIN), 0)
    column = lax.broadcasted_iota(jnp.int32, (DK, WIN), 1)
    for side, copy in enumerate(copies):
        copy.wait()
        at = side * half
        for group in range(GROUPS):
            first = 0 if group == 0 else WIN - DK
            keep = (lane >= first) & (lane < first + DK)
            lo = group * LANES
            k = jnp.where(keep, kv_buf[at:at + half, lo:lo + WIN], jnp.zeros((), jnp.bfloat16))
            kz[group, at:at + half, :] = k
            turn = jnp.where(column == one + first, 1.0, 0.0).astype(jnp.bfloat16)
            kt[group, :, at:at + half] = dot(turn, k, NT).astype(jnp.bfloat16)


def start_copies(owners, h_of, q_hbm, do_hbm, own_hbm, par_hbm, mask_hbm, q_buf, do_buf, kv_buf, mask_buf, sems, others):
    per_owner = q_buf.shape[1]
    keys = [
        pltpu.make_async_copy(own_hbm, kv_buf.at[pl.ds(0, own_hbm.shape[0])], others.at[0]),
        pltpu.make_async_copy(par_hbm, kv_buf.at[pl.ds(own_hbm.shape[0], own_hbm.shape[0])], others.at[1]),
    ]
    mask = pltpu.make_async_copy(mask_hbm, mask_buf, others.at[2])
    for copy in keys:
        copy.start()

    def copies(i, h):
        return (
            pltpu.make_async_copy(q_hbm.at[pl.ds(h, per_owner)], q_buf.at[i], sems.at[0, i]),
            pltpu.make_async_copy(do_hbm.at[pl.ds(h, per_owner)], do_buf.at[i], sems.at[1, i]),
        )

    for i in range(owners):
        for copy in copies(i, h_of(i)):
            copy.start()
        if i == 0:
            mask.start()
    return keys, mask, copies


def group_terms(group, i, h, q_buf, do_buf, lse_ref, delta_ref, mask_ref, kz, kv_buf):
    per_owner, count = q_buf.shape[1:3]
    rows = per_owner * count
    lo = group * LANES
    q = q_buf[i, :, :, lo:lo + WIN].reshape(rows, WIN)
    do = do_buf[i, :, :, lo:lo + DV].reshape(rows, DV)
    lse = jnp.concatenate([lse_ref[group, pl.ds(h + j, 1), :] for j in range(per_owner)], axis=1) * LOG2E
    delta = jnp.concatenate([delta_ref[group, pl.ds(h + j, 1), :] for j in range(per_owner)], axis=1)
    s = dot(kz[group], q, NT)
    vlo = 3 * LANES + lo
    dp = dot(kv_buf[:, vlo:vlo + DV], do, NT)
    p = jnp.exp2(s * (SCALE * LOG2E) - lse) * jnp.concatenate([mask_ref[...]] * per_owner, axis=1)
    ds = (p * (dp - delta)).astype(jnp.bfloat16)
    return q, do, p.astype(jnp.bfloat16), ds


def far_kernel(q_hbm, do_hbm, own_hbm, par_hbm, mask_hbm, lse_ref, delta_ref, right, left,
               q_buf, do_buf, kv_buf, mask_ref, kz, kt, held, sems, others):
    per_owner, _, count = right.shape
    me = lax.axis_index("ka")
    h_of = lambda i: per_owner * lax.rem(me + pick(i, FAR), KA)
    key_copies, mask_copy, copies = start_copies(
        len(FAR), h_of, q_hbm, do_hbm, own_hbm, par_hbm, mask_hbm, q_buf, do_buf, kv_buf, mask_ref, sems, others)
    load_keys(key_copies, kv_buf, kz, kt)
    mask_copy.wait()

    def one(i, carry):
        h = h_of(i)
        for copy in copies(i, h):
            copy.wait()
        for group in range(GROUPS):
            _, _, _, ds = group_terms(group, i, h, q_buf, do_buf, lse_ref, delta_ref, mask_ref, kz, kv_buf)
            dqt = dot(kt[group], ds, NN) * SCALE
            for j in range(per_owner):
                held[i, j, group * DK:(group + 1) * DK, :] = dqt[:, j * count:(j + 1) * count].astype(held.dtype)
        return carry

    lax.fori_loop(0, len(FAR), one, 0)
    width = GROUPS * DK
    right[:, :width, :] = held[0]
    left[:, :width, :] = held[1]
    right[:, width:, :] = held[2, :, :DK, :]
    left[:, width:, :] = held[2, :, DK:, :]


def near_kernel(q_hbm, do_hbm, own_hbm, par_hbm, mask_hbm, lse_ref, delta_ref, after, home, near, own_out, par_out,
                q_buf, do_buf, kv_buf, mask_ref, kz, kt, acc_k, acc_v, near_buf, own_buf, par_buf, sems, others):
    del after
    per_owner, _, count = home.shape
    half = own_out.shape[0]
    me = lax.axis_index("ka")
    steps = NEAR + FAR
    h_of = lambda i: per_owner * lax.rem(me + pick(i, steps), KA)
    key_copies, mask_copy, copies = start_copies(
        KA, h_of, q_hbm, do_hbm, own_hbm, par_hbm, mask_hbm, q_buf, do_buf, kv_buf, mask_ref, sems, others)
    acc_k[...] = jnp.zeros_like(acc_k)
    acc_v[...] = jnp.zeros_like(acc_v)
    load_keys(key_copies, kv_buf, kz, kt)
    mask_copy.wait()

    def one(i, query_grads):
        h = h_of(i)
        for copy in copies(i, h):
            copy.wait()
        for group in range(GROUPS):
            q, do, p, ds = group_terms(group, i, h, q_buf, do_buf, lse_ref, delta_ref, mask_ref, kz, kv_buf)
            acc_v[group] += dot(p, do, NN)
            acc_k[group] += dot(ds, q, NN)
            if query_grads is not None:
                dqt = dot(kt[group], ds, NN) * SCALE
                for j in range(per_owner):
                    query_grads(j, slice(group * DK, (group + 1) * DK), dqt[:, j * count:(j + 1) * count])


    def near_one(i, carry):
        def to_near(j, where, value):
            near_buf[i, j, where, :] = value

        one(i, to_near)
        return carry

    def far_one(i, carry):
        one(i, None)
        return carry

    lax.fori_loop(0, len(NEAR), near_one, 0)
    results = (
        pltpu.make_async_copy(near_buf.at[0], home, others.at[0]),
        pltpu.make_async_copy(near_buf.at[pl.ds(1, len(NEAR) - 1)], near, others.at[1]),
    )
    for copy in results:
        copy.start()
    lax.fori_loop(len(NEAR), KA, far_one, 0)
    low = lax.broadcasted_iota(jnp.int32, (half, LANES), 1) < DK - LANES
    sums = []
    for side, (out, held) in ((1, (par_out, par_buf)), (0, (own_out, own_buf))):
        at = side * half
        a = acc_k[0, at:at + half, :] * SCALE
        b = acc_k[1, at:at + half, :] * SCALE
        held[:, :LANES] = a[:, :LANES].astype(held.dtype)
        held[:, LANES:2 * LANES] = jnp.where(low, a[:, LANES:], b[:, :LANES]).astype(held.dtype)
        held[:, 2 * LANES:3 * LANES] = b[:, LANES:].astype(held.dtype)
        for group in range(GROUPS):
            vlo = (3 + group) * LANES
            held[:, vlo:vlo + DV] = acc_v[group, at:at + half, :].astype(held.dtype)
        sums.append(pltpu.make_async_copy(held, out, others.at[2 + side]))
        sums[-1].start()
    for copy in sums:
        copy.wait()
    for copy in results:
        copy.wait()


def grads(kernel, owners, matmuls, outs, out_specs, scratch, q, do, own, par, mask, lse, delta, *after):
    heads, count, width = q.shape
    per_owner = heads // KA
    keys = 2 * own.shape[0]
    bf16 = jnp.bfloat16
    return pl.pallas_call(
        kernel,
        out_shape=outs,
        in_specs=[HBM] * 5 + [VMEM] * 2 + [HBM] * len(after),
        out_specs=out_specs,
        scratch_shapes=[
            pltpu.VMEM((owners, per_owner, count, width), bf16),
            pltpu.VMEM((owners, per_owner, count, do.shape[2]), bf16),
            pltpu.VMEM((keys, own.shape[1]), bf16),
            pltpu.VMEM(mask.shape, mask.dtype),
            pltpu.VMEM((GROUPS, keys, WIN), bf16),
            pltpu.VMEM((GROUPS, DK, keys), bf16),
            *scratch,
            pltpu.SemaphoreType.DMA((2, owners)),
            pltpu.SemaphoreType.DMA((4,)),
        ],
        cost_estimate=pl.CostEstimate(
            flops=2 * GROUPS * owners * per_owner * count * keys * matmuls, bytes_accessed=6_000_000,
            transcendentals=GROUPS * owners * per_owner * count * keys),
        compiler_params=pltpu.CompilerParams(vmem_limit_bytes=GRANT),
    )(q, do, own, par, mask, lse, delta, *after)


def small(kernel, outs, *args, out_specs=None):
    return pl.pallas_call(
        kernel,
        out_shape=outs,
        in_specs=[VMEM] * len(args),
        out_specs=out_specs or tuple(VMEM for _ in outs),
        compiler_params=pltpu.CompilerParams(vmem_limit_bytes=16 * 1024 * 1024),
    )(*args)


def copies_kernel(keys, values, out, held, sems):
    width = keys.shape[1]
    parts = (
        pltpu.make_async_copy(keys, held.at[:, pl.ds(0, width)], sems.at[0]),
        pltpu.make_async_copy(values, held.at[:, pl.ds(width, values.shape[1])], sems.at[1]),
    )
    for copy in parts:
        copy.start()
    for copy in parts:
        copy.wait()
    sends = [pltpu.make_async_copy(held, out.at[i], sems.at[2 + i]) for i in range(out.shape[0])]
    for copy in sends:
        copy.start()
    for copy in sends:
        copy.wait()


def sum_kernel(own, other, out):
    out[...] = (own[...] + other[...].astype(jnp.float32)).astype(out.dtype)


def message_kernel(near, from_left, from_right, up2, down2, up1, down1, near_buf, left_buf, right_buf, held, sems):
    f32 = jnp.float32
    width = up1.shape[1]
    arrivals = (
        pltpu.make_async_copy(from_left, left_buf, sems.at[0]),
        pltpu.make_async_copy(from_right, right_buf, sems.at[1]),
    )
    terms = [pltpu.make_async_copy(near.at[i], near_buf.at[i], sems.at[2 + i]) for i in range(4)]
    sends = [pltpu.make_async_copy(held.at[i], out, sems.at[6 + i]) for i, out in enumerate((up1, down1, up2, down2))]
    for copy in (arrivals[0], terms[2], arrivals[1], terms[3], terms[0], terms[1]):
        copy.start()
    for i in (2, 3, 0, 1):
        terms[i].wait()
        if i >= 2:
            arrivals[i - 2].wait()
        total = near_buf.at[i]
        if i == 0:
            held[i] = (total[...] + left_buf[:, :width, :].astype(f32)).astype(held.dtype)
        elif i == 1:
            held[i] = (total[...] + right_buf[:, :width, :].astype(f32)).astype(held.dtype)
        elif i == 2:
            held[i, :, :DK, :] = (total[:, :DK, :] + left_buf[:, width:, :].astype(f32)).astype(held.dtype)
            held[i, :, DK:, :] = total[:, DK:, :].astype(held.dtype)
        else:
            held[i, :, :DK, :] = total[:, :DK, :].astype(held.dtype)
            held[i, :, DK:, :] = (total[:, DK:, :] + right_buf[:, width:, :].astype(f32)).astype(held.dtype)
        sends[i].start()
    for copy in sends:
        copy.wait()


def finish_kernel(home, a, b, c, d, pieces, dq, dk, dv):
    f32 = jnp.float32
    for j in range(home.shape[0]):
        total = home[j] + ((a[j].astype(f32) + b[j].astype(f32)) + (c[j].astype(f32) + d[j].astype(f32)))
        dq[j] = total.T
    kv = pieces[0].astype(f32)
    for i in range(1, pieces.shape[0]):
        kv = kv + pieces[i].astype(f32)
    width = dk.shape[1]
    dk[...] = kv[:, :width]
    dv[...] = kv[:, width:]


def per_device(queries, comp_keys, comp_values, outputs, grad_out, log_sums, visible):
    pb = lax.axis_size("pb")
    ka = lax.axis_size("ka")
    chips = pb // 2
    core = lax.rem(lax.axis_index("pb"), 2)
    same_core = [[2 * i + c for i in range(chips)] for c in range(2)]
    other_core = [(i, i ^ 1) for i in range(pb)]
    rows, width = comp_keys.shape
    both = width + comp_values.shape[1]
    heads, count, _ = queries.shape
    per_owner = heads // ka
    keys = 2 * chips * rows
    half = keys // 2
    f32, bf16 = jnp.float32, jnp.bfloat16
    shape = jax.ShapeDtypeStruct

    def along(x, step):
        return lax.ppermute(x, "ka", [(i, (i + step) % ka) for i in range(ka)])

    copies = pl.pallas_call(
        copies_kernel,
        out_shape=shape((chips, rows, both), bf16),
        in_specs=[HBM, HBM],
        out_specs=HBM,
        scratch_shapes=[pltpu.VMEM((rows, both), bf16), pltpu.SemaphoreType.DMA((2 + chips,))],
        compiler_params=pltpu.CompilerParams(vmem_limit_bytes=GRANT),
        name="copies",
    )(comp_keys, comp_values)
    own = lax.all_to_all(copies, "pb", 0, 0, axis_index_groups=same_core, tiled=True).reshape(half, both)
    delta = jnp.stack([
        jnp.sum(
            grad_out[:, :, g * DV:(g + 1) * DV].astype(f32) * outputs[:, :, g * DV:(g + 1) * DV].astype(f32), axis=2
        )
        for g in range(GROUPS)
    ])
    seen = visible.reshape(visible.shape[0], chips, 2, rows)
    seen = jnp.where(core == 0, seen, seen[:, :, ::-1])
    seen = seen.transpose(2, 1, 3, 0).reshape(keys, visible.shape[0])
    mask = jnp.repeat(seen.astype(f32), QBLK, axis=1)
    own, delta, mask = lax.optimization_barrier((own, delta, mask))
    par = lax.ppermute(own, "pb", other_core)

    args = (queries, grad_out, own, par, mask, log_sums, delta)
    hops = shape((per_owner, width + DK, count), bf16)
    chunk = (per_owner, width, count)
    right, left = grads(
        far_kernel, len(FAR), 2 * DK + DV, (hops, hops), (VMEM, VMEM), [pltpu.VMEM((len(FAR), *chunk), bf16)], *args
    )
    from_left = along(right, 2)
    from_right = along(left, -2)
    home, near, own_kv, par_kv = grads(
        near_kernel, KA, 3 * DK + 2 * DV,
        (shape(chunk, f32), shape((len(NEAR) - 1, *chunk), f32), shape((half, both), f32), shape((half, both), bf16)),
        (HBM, HBM, HBM, HBM),
        [
            pltpu.VMEM((GROUPS, keys, WIN), f32),
            pltpu.VMEM((GROUPS, keys, DV), f32),
            pltpu.VMEM((len(NEAR), *chunk), f32),
            pltpu.VMEM((half, both), f32),
            pltpu.VMEM((half, both), bf16),
        ],
        *args, right,
    )
    from_other = lax.ppermute(par_kv, "pb", other_core)

    up2, down2, up1, down1 = pl.pallas_call(
        message_kernel,
        out_shape=(shape(chunk, bf16),) * 4,
        in_specs=[HBM] * 3,
        out_specs=(HBM,) * 4,
        scratch_shapes=[
            pltpu.VMEM(near.shape, f32),
            pltpu.VMEM(hops.shape, bf16),
            pltpu.VMEM(hops.shape, bf16),
            pltpu.VMEM((4, *chunk), bf16),
            pltpu.SemaphoreType.DMA((10,)),
        ],
        compiler_params=pltpu.CompilerParams(vmem_limit_bytes=GRANT),
        name="messages",
    )(near, from_left, from_right)
    from_up2 = along(up2, 2)
    from_down2 = along(down2, -2)
    from_up1 = along(up1, 1)
    from_down1 = along(down1, -1)
    blocks = 4
    block = pl.BlockSpec((half // blocks, both), lambda i: (i, 0))
    chip_sum = pl.pallas_call(
        sum_kernel,
        out_shape=shape((half, both), bf16),
        grid=(blocks,),
        in_specs=[block, block],
        out_specs=block,
        compiler_params=pltpu.CompilerParams(vmem_limit_bytes=GRANT),
        name="chip_sum",
    )(own_kv, from_other)
    pieces = lax.all_to_all(chip_sum.reshape(chips, rows, both), "pb", 0, 0, axis_index_groups=same_core, tiled=True)
    arrived = (from_up2, from_down2, from_up1, from_down1)
    return small(
        finish_kernel,
        (shape((per_owner, count, width), f32), shape((rows, width), f32), shape((rows, both - width), f32)),
        home, *arrived, pieces,
    )


def solution(mesh):
    return jax.shard_map(
        per_device,
        mesh=mesh,
        in_specs=(
            P(None, "pb", "ga"),
            P(("ka", "pb"), "ga"),
            P(("ka", "pb"), "ga"),
            P(None, "pb", "ga"),
            P(None, "pb", "ga"),
            P("ga", None, "pb"),
            P("pb", "ka"),
        ),
        out_specs=(P("ka", "pb", "ga"), P(("ka", "pb"), "ga"), P(("ka", "pb"), "ga")),
        check_vma=False,
    )
```

```python
import math

import jax
import jax.numpy as jnp
from jax import lax
from jax.experimental import pallas as pl
from jax.experimental.pallas import tpu as pltpu
from jax.sharding import PartitionSpec as P


DK = 192
DV = 128
QBLK = 64
LANES = 128
GROUPS = 2
WIN = 256
SCALE = 1.0 / math.sqrt(DK)
LOG2E = math.log2(math.e)
FAR = (3, 5, 4)
NEAR = (0, 1, 7, 2, 6)
KA = 8
GRANT = 20 * 1024 * 1024
NT = (((1,), (1,)), ((), ()))
NN = (((1,), (0,)), ((), ()))
VMEM = pl.BlockSpec(memory_space=pltpu.VMEM)
HBM = pl.BlockSpec(memory_space=pltpu.HBM)


def dot(a, b, dims):
    return lax.dot_general(a, b, dims, preferred_element_type=jnp.float32)


def pick(i, values):
    result = jnp.int32(values[0])
    for n, value in enumerate(values[1:], 1):
        result = jnp.where(i == n, jnp.int32(value), result)
    return result


def load_keys(own_ref, par_ref, kz, vz, kt):
    half = own_ref.shape[0]
    lane = lax.broadcasted_iota(jnp.int32, (half, WIN), 1)
    one = lax.broadcasted_iota(jnp.int32, (DK, WIN), 0)
    column = lax.broadcasted_iota(jnp.int32, (DK, WIN), 1)
    for side, ref in enumerate((own_ref, par_ref)):
        at = side * half
        for group in range(GROUPS):
            first = 0 if group == 0 else WIN - DK
            keep = (lane >= first) & (lane < first + DK)
            lo = group * LANES
            vlo = 3 * LANES + lo
            k = jnp.where(keep, ref[:, lo:lo + WIN], jnp.zeros((), jnp.bfloat16))
            kz[group, at:at + half, :] = k
            vz[group, at:at + half, :] = ref[:, vlo:vlo + DV]
            turn = jnp.where(column == one + first, 1.0, 0.0).astype(jnp.bfloat16)
            kt[group, :, at:at + half] = dot(turn, k, NT).astype(jnp.bfloat16)


def group_terms(group, h, per_owner, q_ref, do_ref, mask_ref, lse_ref, delta_ref, kz, vz):
    rows = per_owner * q_ref.shape[1]
    lo = group * LANES
    q = q_ref[pl.ds(h, per_owner), :, lo:lo + WIN].reshape(rows, WIN)
    do = do_ref[pl.ds(h, per_owner), :, lo:lo + DV].reshape(rows, DV)
    lse = jnp.concatenate([lse_ref[group, pl.ds(h + j, 1), :] for j in range(per_owner)], axis=1) * LOG2E
    delta = jnp.concatenate([delta_ref[group, pl.ds(h + j, 1), :] for j in range(per_owner)], axis=1)
    s = dot(kz[group], q, NT)
    dp = dot(vz[group], do, NT)
    p = jnp.exp2(s * (SCALE * LOG2E) - lse) * jnp.concatenate([mask_ref[...]] * per_owner, axis=1)
    ds = (p * (dp - delta)).astype(jnp.bfloat16)
    return q, do, p.astype(jnp.bfloat16), ds


def far_kernel(q_ref, do_ref, mask_ref, lse_ref, delta_ref, own_ref, par_ref, right, left, kz, vz, kt, held):
    per_owner, _, count = right.shape
    me = lax.axis_index("ka")
    load_keys(own_ref, par_ref, kz, vz, kt)

    def one(i, carry):
        h = per_owner * lax.rem(me + pick(i, FAR), KA)
        for group in range(GROUPS):
            ds = group_terms(group, h, per_owner, q_ref, do_ref, mask_ref, lse_ref, delta_ref, kz, vz)[3]
            dqt = dot(kt[group], ds, NN) * SCALE
            for j in range(per_owner):
                held[i, j, group * DK:(group + 1) * DK, :] = dqt[:, j * count:(j + 1) * count].astype(held.dtype)
        return carry

    lax.fori_loop(0, len(FAR), one, 0)
    width = GROUPS * DK
    right[:, :width, :] = held[0]
    left[:, :width, :] = held[1]
    right[:, width:, :] = held[2, :, :DK, :]
    left[:, width:, :] = held[2, :, DK:, :]


def near_kernel(q_ref, do_ref, mask_ref, lse_ref, delta_ref, kz, vz, kt, near, own_out, par_out, acc_k, acc_v):
    _, per_owner, _, count = near.shape
    half = own_out.shape[0]
    me = lax.axis_index("ka")
    steps = NEAR + FAR
    acc_k[...] = jnp.zeros_like(acc_k)
    acc_v[...] = jnp.zeros_like(acc_v)

    def one(i, query_grads):
        h = per_owner * lax.rem(me + pick(i, steps), KA)
        for group in range(GROUPS):
            q, do, p, ds = group_terms(group, h, per_owner, q_ref, do_ref, mask_ref, lse_ref, delta_ref, kz, vz)
            acc_v[group] += dot(p, do, NN)
            acc_k[group] += dot(ds, q, NN)
            if query_grads:
                dqt = dot(kt[group], ds, NN) * SCALE
                for j in range(per_owner):
                    near[i, j, group * DK:(group + 1) * DK, :] = dqt[:, j * count:(j + 1) * count]

    def near_one(i, carry):
        one(i, True)
        return carry

    def far_one(i, carry):
        one(i, False)
        return carry

    lax.fori_loop(0, len(NEAR), near_one, 0)
    lax.fori_loop(len(NEAR), KA, far_one, 0)
    low = lax.broadcasted_iota(jnp.int32, (half, LANES), 1) < DK - LANES
    for side, out in enumerate((own_out, par_out)):
        at = side * half
        a = acc_k[0, at:at + half, :] * SCALE
        b = acc_k[1, at:at + half, :] * SCALE
        out[:, :LANES] = a[:, :LANES].astype(out.dtype)
        out[:, LANES:2 * LANES] = jnp.where(low, a[:, LANES:], b[:, :LANES]).astype(out.dtype)
        out[:, 2 * LANES:3 * LANES] = b[:, LANES:].astype(out.dtype)
        for group in range(GROUPS):
            vlo = (3 + group) * LANES
            out[:, vlo:vlo + DV] = acc_v[group, at:at + half, :].astype(out.dtype)


def grads(kernel, owners, matmuls, outs, scratch, *args):
    heads, count, _ = args[0].shape
    keys = args[2].shape[0]
    terms = GROUPS * owners * (heads // KA) * count * keys
    return pl.pallas_call(
        kernel,
        out_shape=outs,
        in_specs=[VMEM] * len(args),
        out_specs=tuple(VMEM for _ in outs),
        scratch_shapes=scratch,
        cost_estimate=pl.CostEstimate(flops=2 * terms * matmuls, bytes_accessed=6_000_000, transcendentals=terms),
        compiler_params=pltpu.CompilerParams(vmem_limit_bytes=GRANT),
    )(*args)


def small(kernel, outs, *args):
    return pl.pallas_call(
        kernel,
        out_shape=outs,
        in_specs=[VMEM] * len(args),
        out_specs=tuple(VMEM for _ in outs),
        compiler_params=pltpu.CompilerParams(vmem_limit_bytes=GRANT),
    )(*args)


def copies_kernel(keys, values, out, held, sems):
    width = keys.shape[1]
    parts = (
        pltpu.make_async_copy(keys, held.at[:, pl.ds(0, width)], sems.at[0]),
        pltpu.make_async_copy(values, held.at[:, pl.ds(width, values.shape[1])], sems.at[1]),
    )
    for copy in parts:
        copy.start()
    for copy in parts:
        copy.wait()
    sends = [pltpu.make_async_copy(held, out.at[i], sems.at[2 + i]) for i in range(out.shape[0])]
    for copy in sends:
        copy.start()
    for copy in sends:
        copy.wait()


def message_kernel(near, from_left, from_right, up2, down2, up1, down1):
    f32, bf16 = jnp.float32, jnp.bfloat16
    width = up1.shape[1]
    up1[...] = (near[1] + from_left[:, :width, :].astype(f32)).astype(bf16)
    down1[...] = (near[2] + from_right[:, :width, :].astype(f32)).astype(bf16)
    up2[:, :DK, :] = (near[3, :, :DK, :] + from_left[:, width:, :].astype(f32)).astype(bf16)
    up2[:, DK:, :] = near[3, :, DK:, :].astype(bf16)
    down2[:, :DK, :] = near[4, :, :DK, :].astype(bf16)
    down2[:, DK:, :] = (near[4, :, DK:, :] + from_right[:, width:, :].astype(f32)).astype(bf16)


def finish_kernel(near, a, b, c, d, pieces, dq, dk, dv):
    f32 = jnp.float32
    for j in range(near.shape[1]):
        total = near[0, j] + ((a[j].astype(f32) + b[j].astype(f32)) + (c[j].astype(f32) + d[j].astype(f32)))
        dq[j] = total.T
    kv = pieces[0].astype(f32)
    for i in range(1, pieces.shape[0]):
        kv = kv + pieces[i].astype(f32)
    width = dk.shape[1]
    dk[...] = kv[:, :width]
    dv[...] = kv[:, width:]


def per_device(queries, comp_keys, comp_values, outputs, grad_out, log_sums, visible):
    pb = lax.axis_size("pb")
    ka = lax.axis_size("ka")
    chips = pb // 2
    core = lax.rem(lax.axis_index("pb"), 2)
    same_core = [[2 * i + c for i in range(chips)] for c in range(2)]
    other_core = [(i, i ^ 1) for i in range(pb)]
    rows, width = comp_keys.shape
    both = width + comp_values.shape[1]
    heads, count, _ = queries.shape
    per_owner = heads // ka
    keys = 2 * chips * rows
    half = keys // 2
    f32, bf16 = jnp.float32, jnp.bfloat16
    shape = jax.ShapeDtypeStruct

    def along(x, step):
        return lax.ppermute(x, "ka", [(i, (i + step) % ka) for i in range(ka)])

    copies = pl.pallas_call(
        copies_kernel,
        out_shape=shape((chips, rows, both), bf16),
        in_specs=[HBM, HBM],
        out_specs=HBM,
        scratch_shapes=[pltpu.VMEM((rows, both), bf16), pltpu.SemaphoreType.DMA((2 + chips,))],
        compiler_params=pltpu.CompilerParams(vmem_limit_bytes=GRANT),
        name="copies",
    )(comp_keys, comp_values)
    own = lax.all_to_all(copies, "pb", 0, 0, axis_index_groups=same_core, tiled=True).reshape(half, both)
    delta = jnp.stack([
        jnp.sum(
            grad_out[:, :, g * DV:(g + 1) * DV].astype(f32) * outputs[:, :, g * DV:(g + 1) * DV].astype(f32), axis=2
        )
        for g in range(GROUPS)
    ])
    seen = visible.reshape(visible.shape[0], chips, 2, rows)
    seen = jnp.where(core == 0, seen, seen[:, :, ::-1])
    seen = seen.transpose(2, 1, 3, 0).reshape(keys, visible.shape[0])
    mask = jnp.repeat(seen.astype(f32), QBLK, axis=1)
    own, delta, mask = lax.optimization_barrier((own, delta, mask))
    par = lax.ppermute(own, "pb", other_core)

    args = (queries, grad_out, mask, log_sums, delta)
    hops = shape((per_owner, width + DK, count), bf16)
    chunk = (per_owner, width, count)
    right, left, kz, vz, kt = grads(
        far_kernel, len(FAR), 2 * DK + DV,
        (
            hops, hops, shape((GROUPS, keys, WIN), bf16), shape((GROUPS, keys, DV), bf16),
            shape((GROUPS, DK, keys), bf16),
        ),
        [pltpu.VMEM((len(FAR), *chunk), bf16)], *args, own, par,
    )
    from_left = along(right, 2)
    from_right = along(left, -2)
    near, own_kv, par_kv = grads(
        near_kernel, KA, 3 * DK + 2 * DV,
        (shape((len(NEAR), *chunk), f32), shape((half, both), f32), shape((half, both), bf16)),
        [pltpu.VMEM((GROUPS, keys, WIN), f32), pltpu.VMEM((GROUPS, keys, DV), f32)], *args, kz, vz, kt,
    )
    from_other = lax.ppermute(par_kv, "pb", other_core)

    up2, down2, up1, down1 = small(message_kernel, (shape(chunk, bf16),) * 4, near, from_left, from_right)
    from_up2 = along(up2, 2)
    from_down2 = along(down2, -2)
    from_up1 = along(up1, 1)
    from_down1 = along(down1, -1)
    chip_sum = (own_kv + from_other.astype(f32)).astype(bf16)
    pieces = lax.all_to_all(chip_sum.reshape(chips, rows, both), "pb", 0, 0, axis_index_groups=same_core, tiled=True)
    arrived = (from_up2, from_down2, from_up1, from_down1)
    return small(
        finish_kernel,
        (shape((per_owner, count, width), f32), shape((rows, width), f32), shape((rows, both - width), f32)),
        near, *arrived, pieces,
    )


def solution(mesh):
    return jax.shard_map(
        per_device,
        mesh=mesh,
        in_specs=(
            P(None, "pb", "ga"),
            P(("ka", "pb"), "ga"),
            P(("ka", "pb"), "ga"),
            P(None, "pb", "ga"),
            P(None, "pb", "ga"),
            P("ga", None, "pb"),
            P("pb", "ka"),
        ),
        out_specs=(P("ka", "pb", "ga"), P(("ka", "pb"), "ga"), P(("ka", "pb"), "ga")),
        check_vma=False,
    )
```

```python
import math

import jax
import jax.numpy as jnp
from jax import lax
from jax.experimental import pallas as pl
from jax.experimental.pallas import tpu as pltpu
from jax.sharding import PartitionSpec as P


DK = 192
DV = 128
QBLK = 64
LANES = 128
GROUPS = 2
WIN = 256
SCALE = 1.0 / math.sqrt(DK)
LOG2E = math.log2(math.e)
FAR = (3, 5, 4)
NEAR = (0, 1, 7, 2, 6)
KA = 8
GRANT = 20 * 1024 * 1024
NT = (((1,), (1,)), ((), ()))
NN = (((1,), (0,)), ((), ()))
VMEM = pl.BlockSpec(memory_space=pltpu.VMEM)
HBM = pl.BlockSpec(memory_space=pltpu.HBM)


def dot(a, b, dims):
    return lax.dot_general(a, b, dims, preferred_element_type=jnp.float32)


def pick(i, values):
    result = jnp.int32(values[0])
    for n, value in enumerate(values[1:], 1):
        result = jnp.where(i == n, jnp.int32(value), result)
    return result


def load_keys(ref, at, kz, vz, kt):
    half = ref.shape[0]
    lane = lax.broadcasted_iota(jnp.int32, (half, WIN), 1)
    one = lax.broadcasted_iota(jnp.int32, (DK, WIN), 0)
    column = lax.broadcasted_iota(jnp.int32, (DK, WIN), 1)
    for group in range(GROUPS):
        first = 0 if group == 0 else WIN - DK
        keep = (lane >= first) & (lane < first + DK)
        lo = group * LANES
        vlo = 3 * LANES + lo
        k = jnp.where(keep, ref[:, lo:lo + WIN], jnp.zeros((), jnp.bfloat16))
        kz[group, at:at + half, :] = k
        vz[group, at:at + half, :] = ref[:, vlo:vlo + DV]
        turn = jnp.where(column == one + first, 1.0, 0.0).astype(jnp.bfloat16)
        kt[group, :, at:at + half] = dot(turn, k, NT).astype(jnp.bfloat16)


def group_terms(group, keys, h, q_at, per_owner, q_ref, do_ref, mask_ref, lse_ref, delta_ref, kz, vz):
    rows = per_owner * q_ref.shape[1]
    lo = group * LANES
    q = q_ref[pl.ds(q_at, per_owner), :, lo:lo + WIN].reshape(rows, WIN)
    do = do_ref[pl.ds(h, per_owner), :, lo:lo + DV].reshape(rows, DV)
    lse = jnp.concatenate([lse_ref[group, pl.ds(h + j, 1), :] for j in range(per_owner)], axis=1) * LOG2E
    delta = jnp.concatenate([delta_ref[group, pl.ds(h + j, 1), :] for j in range(per_owner)], axis=1)
    s = dot(kz[group, keys, :], q, NT)
    dp = dot(vz[group, keys, :], do, NT)
    p = jnp.exp2(s * (SCALE * LOG2E) - lse) * jnp.concatenate([mask_ref[keys, :]] * per_owner, axis=1)
    ds = (p * (dp - delta)).astype(jnp.bfloat16)
    return q, do, p.astype(jnp.bfloat16), ds


def far_terms(side, args, key_ref, kz, vz, kt, emit):
    per_owner = args[0].shape[0] // len(FAR)
    count = args[0].shape[1]
    half = key_ref.shape[0]
    at = side * half
    me = lax.axis_index("ka")
    load_keys(key_ref, at, kz, vz, kt)

    def one(i, carry):
        h = per_owner * lax.rem(me + pick(i, FAR), KA)
        for group in range(GROUPS):
            ds = group_terms(group, slice(at, at + half), h, per_owner * i, per_owner, *args, kz, vz)[3]
            dqt = dot(kt[group, :, at:at + half], ds, NN)
            for j in range(per_owner):
                emit(i, j, slice(group * DK, (group + 1) * DK), dqt[:, j * count:(j + 1) * count])
        return carry

    lax.fori_loop(0, len(FAR), one, 0)


def far_own_kernel(q_ref, do_ref, mask_ref, lse_ref, delta_ref, own_ref, partial, kz, vz, kt):
    def emit(i, j, where, value):
        partial[i, j, where, :] = value

    far_terms(0, (q_ref, do_ref, mask_ref, lse_ref, delta_ref), own_ref, kz, vz, kt, emit)


def far_par_kernel(q_ref, do_ref, mask_ref, lse_ref, delta_ref, par_ref, partial, in_kz, in_vz, in_kt,
                   right, left, kz, vz, kt, held):
    del in_kz, in_vz, in_kt

    def emit(i, j, where, value):
        held[i, j, where, :] = ((partial[i, j, where, :] + value) * SCALE).astype(held.dtype)

    far_terms(1, (q_ref, do_ref, mask_ref, lse_ref, delta_ref), par_ref, kz, vz, kt, emit)
    width = GROUPS * DK
    right[:, :width, :] = held[0]
    left[:, :width, :] = held[1]
    right[:, width:, :] = held[2, :, :DK, :]
    left[:, width:, :] = held[2, :, DK:, :]


def near_kernel(q_ref, do_ref, mask_ref, lse_ref, delta_ref, kz, vz, kt, near, own_out, par_out, acc_k, acc_v):
    _, per_owner, _, count = near.shape
    half = own_out.shape[0]
    me = lax.axis_index("ka")
    steps = NEAR + FAR
    acc_k[...] = jnp.zeros_like(acc_k)
    acc_v[...] = jnp.zeros_like(acc_v)

    def one(i, query_grads):
        h = per_owner * lax.rem(me + pick(i, steps), KA)
        for group in range(GROUPS):
            q, do, p, ds = group_terms(
                group, slice(None), h, h, per_owner, q_ref, do_ref, mask_ref, lse_ref, delta_ref, kz, vz)
            acc_v[group] += dot(p, do, NN)
            acc_k[group] += dot(ds, q, NN)
            if query_grads:
                dqt = dot(kt[group], ds, NN) * SCALE
                for j in range(per_owner):
                    near[i, j, group * DK:(group + 1) * DK, :] = dqt[:, j * count:(j + 1) * count]

    def near_one(i, carry):
        one(i, True)
        return carry

    def far_one(i, carry):
        one(i, False)
        return carry

    lax.fori_loop(0, len(NEAR), near_one, 0)
    lax.fori_loop(len(NEAR), KA, far_one, 0)
    low = lax.broadcasted_iota(jnp.int32, (half, LANES), 1) < DK - LANES
    for side, out in enumerate((own_out, par_out)):
        at = side * half
        a = acc_k[0, at:at + half, :] * SCALE
        b = acc_k[1, at:at + half, :] * SCALE
        out[:, :LANES] = a[:, :LANES].astype(out.dtype)
        out[:, LANES:2 * LANES] = jnp.where(low, a[:, LANES:], b[:, :LANES]).astype(out.dtype)
        out[:, 2 * LANES:3 * LANES] = b[:, LANES:].astype(out.dtype)
        for group in range(GROUPS):
            vlo = (3 + group) * LANES
            out[:, vlo:vlo + DV] = acc_v[group, at:at + half, :].astype(out.dtype)


def grads(kernel, rows, keys, matmuls, outs, scratch, *args, aliases=None):
    terms = GROUPS * rows * keys
    return pl.pallas_call(
        kernel,
        out_shape=outs,
        in_specs=[VMEM] * len(args),
        out_specs=tuple(VMEM for _ in outs),
        scratch_shapes=scratch,
        input_output_aliases=aliases or {},
        cost_estimate=pl.CostEstimate(flops=2 * terms * matmuls, bytes_accessed=6_000_000, transcendentals=terms),
        compiler_params=pltpu.CompilerParams(vmem_limit_bytes=GRANT),
    )(*args)


def small(kernel, outs, *args):
    return pl.pallas_call(
        kernel,
        out_shape=outs,
        in_specs=[VMEM] * len(args),
        out_specs=tuple(VMEM for _ in outs),
        compiler_params=pltpu.CompilerParams(vmem_limit_bytes=GRANT),
    )(*args)


def copies_kernel(keys, values, out, held, sems):
    width = keys.shape[1]
    parts = (
        pltpu.make_async_copy(keys, held.at[:, pl.ds(0, width)], sems.at[0]),
        pltpu.make_async_copy(values, held.at[:, pl.ds(width, values.shape[1])], sems.at[1]),
    )
    for copy in parts:
        copy.start()
    for copy in parts:
        copy.wait()
    sends = [pltpu.make_async_copy(held, out.at[i], sems.at[2 + i]) for i in range(out.shape[0])]
    for copy in sends:
        copy.start()
    for copy in sends:
        copy.wait()


def message_kernel(near, from_left, from_right, up2, down2, up1, down1):
    f32, bf16 = jnp.float32, jnp.bfloat16
    width = up1.shape[1]
    up1[...] = (near[1] + from_left[:, :width, :].astype(f32)).astype(bf16)
    down1[...] = (near[2] + from_right[:, :width, :].astype(f32)).astype(bf16)
    up2[:, :DK, :] = (near[3, :, :DK, :] + from_left[:, width:, :].astype(f32)).astype(bf16)
    up2[:, DK:, :] = near[3, :, DK:, :].astype(bf16)
    down2[:, :DK, :] = near[4, :, :DK, :].astype(bf16)
    down2[:, DK:, :] = (near[4, :, DK:, :] + from_right[:, width:, :].astype(f32)).astype(bf16)


def finish_kernel(near, a, b, c, d, pieces, dq, dk, dv):
    f32 = jnp.float32
    for j in range(near.shape[1]):
        total = near[0, j] + ((a[j].astype(f32) + b[j].astype(f32)) + (c[j].astype(f32) + d[j].astype(f32)))
        dq[j] = total.T
    kv = pieces[0].astype(f32)
    for i in range(1, pieces.shape[0]):
        kv = kv + pieces[i].astype(f32)
    width = dk.shape[1]
    dk[...] = kv[:, :width]
    dv[...] = kv[:, width:]


def per_device(queries, comp_keys, comp_values, outputs, grad_out, log_sums, visible):
    pb = lax.axis_size("pb")
    ka = lax.axis_size("ka")
    chips = pb // 2
    core = lax.rem(lax.axis_index("pb"), 2)
    same_core = [[2 * i + c for i in range(chips)] for c in range(2)]
    other_core = [(i, i ^ 1) for i in range(pb)]
    rows, width = comp_keys.shape
    both = width + comp_values.shape[1]
    heads, count, _ = queries.shape
    per_owner = heads // ka
    keys = 2 * chips * rows
    half = keys // 2
    f32, bf16 = jnp.float32, jnp.bfloat16
    shape = jax.ShapeDtypeStruct

    def along(x, step):
        return lax.ppermute(x, "ka", [(i, (i + step) % ka) for i in range(ka)])

    copies = pl.pallas_call(
        copies_kernel,
        out_shape=shape((chips, rows, both), bf16),
        in_specs=[HBM, HBM],
        out_specs=HBM,
        scratch_shapes=[pltpu.VMEM((rows, both), bf16), pltpu.SemaphoreType.DMA((2 + chips,))],
        compiler_params=pltpu.CompilerParams(vmem_limit_bytes=67_000_000),
        name="copies",
    )(comp_keys, comp_values)
    own = lax.all_to_all(copies, "pb", 0, 0, axis_index_groups=same_core, tiled=True).reshape(half, both)
    delta = jnp.stack([
        jnp.sum(
            grad_out[:, :, g * DV:(g + 1) * DV].astype(f32) * outputs[:, :, g * DV:(g + 1) * DV].astype(f32), axis=2
        )
        for g in range(GROUPS)
    ])
    seen = visible.reshape(visible.shape[0], chips, 2, rows)
    seen = jnp.where(core == 0, seen, seen[:, :, ::-1])
    seen = seen.transpose(2, 1, 3, 0).reshape(keys, visible.shape[0])
    mask = jnp.repeat(seen.astype(f32), QBLK, axis=1)
    me = lax.axis_index("ka")
    far_q = jnp.concatenate([
        lax.dynamic_slice_in_dim(queries, per_owner * lax.rem(me + step, ka), per_owner, 0) for step in FAR
    ])
    own, delta, mask, far_q = lax.optimization_barrier((own, delta, mask, far_q))
    par = lax.ppermute(own, "pb", other_core)

    rest = (grad_out, mask, log_sums, delta)
    hops = shape((per_owner, width + DK, count), bf16)
    chunk = (per_owner, width, count)
    key_forms = (
        shape((GROUPS, keys, WIN), bf16), shape((GROUPS, keys, DV), bf16), shape((GROUPS, DK, keys), bf16)
    )
    far_rows = len(FAR) * per_owner * count
    partial, kz, vz, kt = grads(
        far_own_kernel, far_rows, half, 2 * DK + DV, (shape((len(FAR), *chunk), f32), *key_forms), [],
        far_q, *rest, own,
    )
    right, left, kz, vz, kt = grads(
        far_par_kernel, far_rows, half, 2 * DK + DV, (hops, hops, *key_forms),
        [pltpu.VMEM((len(FAR), *chunk), bf16)], far_q, *rest, par, partial, kz, vz, kt, aliases={7: 2, 8: 3, 9: 4},
    )
    from_left = along(right, 2)
    from_right = along(left, -2)
    near, own_kv, par_kv = grads(
        near_kernel, heads * count, keys, 3 * DK + 2 * DV,
        (shape((len(NEAR), *chunk), f32), shape((half, both), f32), shape((half, both), bf16)),
        [pltpu.VMEM((GROUPS, keys, WIN), f32), pltpu.VMEM((GROUPS, keys, DV), f32)], queries, *rest, kz, vz, kt,
    )
    from_other = lax.ppermute(par_kv, "pb", other_core)

    up2, down2, up1, down1 = small(message_kernel, (shape(chunk, bf16),) * 4, near, from_left, from_right)
    from_up2 = along(up2, 2)
    from_down2 = along(down2, -2)
    from_up1 = along(up1, 1)
    from_down1 = along(down1, -1)
    chip_sum = (own_kv + from_other.astype(f32)).astype(bf16)
    pieces = lax.all_to_all(chip_sum.reshape(chips, rows, both), "pb", 0, 0, axis_index_groups=same_core, tiled=True)
    arrived = (from_up2, from_down2, from_up1, from_down1)
    return small(
        finish_kernel,
        (shape((per_owner, count, width), f32), shape((rows, width), f32), shape((rows, both - width), f32)),
        near, *arrived, pieces,
    )


def solution(mesh):
    return jax.shard_map(
        per_device,
        mesh=mesh,
        in_specs=(
            P(None, "pb", "ga"),
            P(("ka", "pb"), "ga"),
            P(("ka", "pb"), "ga"),
            P(None, "pb", "ga"),
            P(None, "pb", "ga"),
            P("ga", None, "pb"),
            P("pb", "ka"),
        ),
        out_specs=(P("ka", "pb", "ga"), P(("ka", "pb"), "ga"), P(("ka", "pb"), "ga")),
        check_vma=False,
    )
```

```python
import math

import jax
import jax.numpy as jnp
from jax import lax
from jax.experimental import pallas as pl
from jax.experimental.pallas import tpu as pltpu
from jax.sharding import PartitionSpec as P


DK = 192
DV = 128
QBLK = 64
LANES = 128
GROUPS = 2
WIN = 256
SCALE = 1.0 / math.sqrt(DK)
LOG2E = math.log2(math.e)
FAR = (3, 5, 4)
NEAR = (0, 1, 7, 2, 6)
KA = 8
COPIES_GRANT = 67_000_000
GRANT = 20 * 1024 * 1024
NT = (((1,), (1,)), ((), ()))
NN = (((1,), (0,)), ((), ()))
VMEM = pl.BlockSpec(memory_space=pltpu.VMEM)
HBM = pl.BlockSpec(memory_space=pltpu.HBM)


def dot(a, b, dims):
    return lax.dot_general(a, b, dims, preferred_element_type=jnp.float32)


def pick(i, values):
    result = jnp.int32(values[0])
    for n, value in enumerate(values[1:], 1):
        result = jnp.where(i == n, jnp.int32(value), result)
    return result


def load_keys(own_ref, par_ref, kz, vz, kt):
    half = own_ref.shape[0]
    lane = lax.broadcasted_iota(jnp.int32, (half, WIN), 1)
    one = lax.broadcasted_iota(jnp.int32, (DK, WIN), 0)
    column = lax.broadcasted_iota(jnp.int32, (DK, WIN), 1)
    for side, ref in enumerate((own_ref, par_ref)):
        at = side * half
        for group in range(GROUPS):
            first = 0 if group == 0 else WIN - DK
            keep = (lane >= first) & (lane < first + DK)
            lo = group * LANES
            vlo = 3 * LANES + lo
            k = jnp.where(keep, ref[:, lo:lo + WIN], jnp.zeros((), jnp.bfloat16))
            kz[group, at:at + half, :] = k
            vz[group, at:at + half, :] = ref[:, vlo:vlo + DV]
            turn = jnp.where(column == one + first, 1.0, 0.0).astype(jnp.bfloat16)
            kt[group, :, at:at + half] = dot(turn, k, NT).astype(jnp.bfloat16)


def group_terms(group, h, q_at, per_owner, q_ref, do_ref, mask_ref, lse_ref, delta_ref, kz, vz):
    rows = per_owner * q_ref.shape[1]
    lo = group * LANES
    q = q_ref[pl.ds(q_at, per_owner), :, lo:lo + WIN].reshape(rows, WIN)
    do = do_ref[pl.ds(h, per_owner), :, lo:lo + DV].reshape(rows, DV)
    lse = jnp.concatenate([lse_ref[group, pl.ds(h + j, 1), :] for j in range(per_owner)], axis=1) * LOG2E
    delta = jnp.concatenate([delta_ref[group, pl.ds(h + j, 1), :] for j in range(per_owner)], axis=1)
    s = dot(kz[group], q, NT)
    dp = dot(vz[group], do, NT)
    p = jnp.exp2(s * (SCALE * LOG2E) - lse) * jnp.concatenate([mask_ref[...]] * per_owner, axis=1)
    ds = (p * (dp - delta)).astype(jnp.bfloat16)
    return q, do, p.astype(jnp.bfloat16), ds


def far_kernel(q_ref, do_ref, mask_ref, lse_ref, delta_ref, own_ref, par_ref, right, left, kz, vz, kt, held):
    per_owner, _, count = right.shape
    me = lax.axis_index("ka")
    load_keys(own_ref, par_ref, kz, vz, kt)

    def one(i, carry):
        h = per_owner * lax.rem(me + pick(i, FAR), KA)
        for group in range(GROUPS):
            ds = group_terms(
                group, h, per_owner * i, per_owner, q_ref, do_ref, mask_ref, lse_ref, delta_ref, kz, vz)[3]
            dqt = dot(kt[group], ds, NN) * SCALE
            for j in range(per_owner):
                held[i, j, group * DK:(group + 1) * DK, :] = dqt[:, j * count:(j + 1) * count].astype(held.dtype)
        return carry

    lax.fori_loop(0, len(FAR), one, 0)
    width = GROUPS * DK
    right[:, :width, :] = held[0]
    left[:, :width, :] = held[1]
    right[:, width:, :] = held[2, :, :DK, :]
    left[:, width:, :] = held[2, :, DK:, :]


def near_kernel(q_ref, do_ref, mask_ref, lse_ref, delta_ref, kz, vz, kt, near, own_out, par_out, acc_k, acc_v):
    _, per_owner, _, count = near.shape
    half = own_out.shape[0]
    me = lax.axis_index("ka")
    steps = NEAR + FAR
    acc_k[...] = jnp.zeros_like(acc_k)
    acc_v[...] = jnp.zeros_like(acc_v)

    def one(i, query_grads):
        h = per_owner * lax.rem(me + pick(i, steps), KA)
        for group in range(GROUPS):
            q, do, p, ds = group_terms(group, h, h, per_owner, q_ref, do_ref, mask_ref, lse_ref, delta_ref, kz, vz)
            acc_v[group] += dot(p, do, NN)
            acc_k[group] += dot(ds, q, NN)
            if query_grads:
                dqt = dot(kt[group], ds, NN) * SCALE
                for j in range(per_owner):
                    near[i, j, group * DK:(group + 1) * DK, :] = dqt[:, j * count:(j + 1) * count]

    def near_one(i, carry):
        one(i, True)
        return carry

    def far_one(i, carry):
        one(i, False)
        return carry

    lax.fori_loop(0, len(NEAR), near_one, 0)
    lax.fori_loop(len(NEAR), KA, far_one, 0)
    low = lax.broadcasted_iota(jnp.int32, (half, LANES), 1) < DK - LANES
    for side, out in enumerate((own_out, par_out)):
        at = side * half
        a = acc_k[0, at:at + half, :] * SCALE
        b = acc_k[1, at:at + half, :] * SCALE
        out[:, :LANES] = a[:, :LANES].astype(out.dtype)
        out[:, LANES:2 * LANES] = jnp.where(low, a[:, LANES:], b[:, :LANES]).astype(out.dtype)
        out[:, 2 * LANES:3 * LANES] = b[:, LANES:].astype(out.dtype)
        for group in range(GROUPS):
            vlo = (3 + group) * LANES
            out[:, vlo:vlo + DV] = acc_v[group, at:at + half, :].astype(out.dtype)


def grads(kernel, rows, keys, matmuls, outs, scratch, *args):
    terms = GROUPS * rows * keys
    return pl.pallas_call(
        kernel,
        out_shape=outs,
        in_specs=[VMEM] * len(args),
        out_specs=tuple(VMEM for _ in outs),
        scratch_shapes=scratch,
        cost_estimate=pl.CostEstimate(flops=2 * terms * matmuls, bytes_accessed=6_000_000, transcendentals=terms),
        compiler_params=pltpu.CompilerParams(vmem_limit_bytes=GRANT),
    )(*args)


def small(kernel, outs, *args):
    return pl.pallas_call(
        kernel,
        out_shape=outs,
        in_specs=[VMEM] * len(args),
        out_specs=tuple(VMEM for _ in outs),
        compiler_params=pltpu.CompilerParams(vmem_limit_bytes=GRANT),
    )(*args)


def copies_kernel(keys, values, out, held, sems):
    width = keys.shape[1]
    parts = (
        pltpu.make_async_copy(keys, held.at[:, pl.ds(0, width)], sems.at[0]),
        pltpu.make_async_copy(values, held.at[:, pl.ds(width, values.shape[1])], sems.at[1]),
    )
    for copy in parts:
        copy.start()
    for copy in parts:
        copy.wait()
    sends = [pltpu.make_async_copy(held, out.at[i], sems.at[2 + i]) for i in range(out.shape[0])]
    for copy in sends:
        copy.start()
    for copy in sends:
        copy.wait()


def message_kernel(near, from_left, from_right, up2, down2, up1, down1):
    f32, bf16 = jnp.float32, jnp.bfloat16
    width = up1.shape[1]
    up1[...] = (near[1] + from_left[:, :width, :].astype(f32)).astype(bf16)
    down1[...] = (near[2] + from_right[:, :width, :].astype(f32)).astype(bf16)
    up2[:, :DK, :] = (near[3, :, :DK, :] + from_left[:, width:, :].astype(f32)).astype(bf16)
    up2[:, DK:, :] = near[3, :, DK:, :].astype(bf16)
    down2[:, :DK, :] = near[4, :, :DK, :].astype(bf16)
    down2[:, DK:, :] = (near[4, :, DK:, :] + from_right[:, width:, :].astype(f32)).astype(bf16)


def finish_kernel(near, a, b, c, d, pieces, dq, dk, dv):
    f32 = jnp.float32
    for j in range(near.shape[1]):
        total = near[0, j] + ((a[j].astype(f32) + b[j].astype(f32)) + (c[j].astype(f32) + d[j].astype(f32)))
        dq[j] = total.T
    kv = pieces[0].astype(f32)
    for i in range(1, pieces.shape[0]):
        kv = kv + pieces[i].astype(f32)
    width = dk.shape[1]
    dk[...] = kv[:, :width]
    dv[...] = kv[:, width:]


def per_device(queries, comp_keys, comp_values, outputs, grad_out, log_sums, visible):
    pb = lax.axis_size("pb")
    ka = lax.axis_size("ka")
    chips = pb // 2
    core = lax.rem(lax.axis_index("pb"), 2)
    same_core = [[2 * i + c for i in range(chips)] for c in range(2)]
    other_core = [(i, i ^ 1) for i in range(pb)]
    rows, width = comp_keys.shape
    both = width + comp_values.shape[1]
    heads, count, _ = queries.shape
    per_owner = heads // ka
    keys = 2 * chips * rows
    half = keys // 2
    f32, bf16 = jnp.float32, jnp.bfloat16
    shape = jax.ShapeDtypeStruct

    def along(x, step):
        return lax.ppermute(x, "ka", [(i, (i + step) % ka) for i in range(ka)])

    copies = pl.pallas_call(
        copies_kernel,
        out_shape=shape((chips, rows, both), bf16),
        in_specs=[HBM, HBM],
        out_specs=HBM,
        scratch_shapes=[pltpu.VMEM((rows, both), bf16), pltpu.SemaphoreType.DMA((2 + chips,))],
        compiler_params=pltpu.CompilerParams(vmem_limit_bytes=COPIES_GRANT),
        name="copies",
    )(comp_keys, comp_values)
    own = lax.all_to_all(copies, "pb", 0, 0, axis_index_groups=same_core, tiled=True).reshape(half, both)
    delta = jnp.stack([
        jnp.sum(
            grad_out[:, :, g * DV:(g + 1) * DV].astype(f32) * outputs[:, :, g * DV:(g + 1) * DV].astype(f32), axis=2
        )
        for g in range(GROUPS)
    ])
    seen = visible.reshape(visible.shape[0], chips, 2, rows)
    seen = jnp.where(core == 0, seen, seen[:, :, ::-1])
    seen = seen.transpose(2, 1, 3, 0).reshape(keys, visible.shape[0])
    mask = jnp.repeat(seen.astype(f32), QBLK, axis=1)
    me = lax.axis_index("ka")
    far_q = jnp.concatenate([
        lax.dynamic_slice_in_dim(queries, per_owner * lax.rem(me + step, ka), per_owner, 0) for step in FAR
    ])
    own, delta, mask, far_q = lax.optimization_barrier((own, delta, mask, far_q))
    par = lax.ppermute(own, "pb", other_core)

    args = (grad_out, mask, log_sums, delta)
    hops = shape((per_owner, width + DK, count), bf16)
    chunk = (per_owner, width, count)
    right, left, kz, vz, kt = grads(
        far_kernel, len(FAR) * per_owner * count, keys, 2 * DK + DV,
        (
            hops, hops, shape((GROUPS, keys, WIN), bf16), shape((GROUPS, keys, DV), bf16),
            shape((GROUPS, DK, keys), bf16),
        ),
        [pltpu.VMEM((len(FAR), *chunk), bf16)], far_q, *args, own, par,
    )
    from_left = along(right, 2)
    from_right = along(left, -2)
    near, own_kv, par_kv = grads(
        near_kernel, heads * count, keys, 3 * DK + 2 * DV,
        (shape((len(NEAR), *chunk), f32), shape((half, both), f32), shape((half, both), bf16)),
        [pltpu.VMEM((GROUPS, keys, WIN), f32), pltpu.VMEM((GROUPS, keys, DV), f32)], queries, *args, kz, vz, kt,
    )
    from_other = lax.ppermute(par_kv, "pb", other_core)

    up2, down2, up1, down1 = small(message_kernel, (shape(chunk, bf16),) * 4, near, from_left, from_right)
    from_up2 = along(up2, 2)
    from_down2 = along(down2, -2)
    from_up1 = along(up1, 1)
    from_down1 = along(down1, -1)
    chip_sum = (own_kv + from_other.astype(f32)).astype(bf16)
    pieces = lax.all_to_all(chip_sum.reshape(chips, rows, both), "pb", 0, 0, axis_index_groups=same_core, tiled=True)
    arrived = (from_up2, from_down2, from_up1, from_down1)
    return small(
        finish_kernel,
        (shape((per_owner, count, width), f32), shape((rows, width), f32), shape((rows, both - width), f32)),
        near, *arrived, pieces,
    )


def solution(mesh):
    return jax.shard_map(
        per_device,
        mesh=mesh,
        in_specs=(
            P(None, "pb", "ga"),
            P(("ka", "pb"), "ga"),
            P(("ka", "pb"), "ga"),
            P(None, "pb", "ga"),
            P(None, "pb", "ga"),
            P("ga", None, "pb"),
            P("pb", "ka"),
        ),
        out_specs=(P("ka", "pb", "ga"), P(("ka", "pb"), "ga"), P(("ka", "pb"), "ga")),
        check_vma=False,
    )
```

```python
import math

import jax
import jax.numpy as jnp
from jax import lax
from jax.experimental import pallas as pl
from jax.experimental.pallas import tpu as pltpu
from jax.sharding import PartitionSpec as P


DK = 192
DV = 128
QBLK = 64
LANES = 128
GROUPS = 2
WIN = 256
SCALE = 1.0 / math.sqrt(DK)
LOG2E = math.log2(math.e)
FAR = (3, 5, 4)
NEAR = (0, 1, 7, 2, 6)
KA = 8
COPIES_GRANT = 67_000_000
GRANT = 20 * 1024 * 1024
NT = (((1,), (1,)), ((), ()))
NN = (((1,), (0,)), ((), ()))
TN = (((0,), (0,)), ((), ()))
VMEM = pl.BlockSpec(memory_space=pltpu.VMEM)
HBM = pl.BlockSpec(memory_space=pltpu.HBM)


def dot(a, b, dims):
    return lax.dot_general(a, b, dims, preferred_element_type=jnp.float32)


def pick(i, values):
    result = jnp.int32(values[0])
    for n, value in enumerate(values[1:], 1):
        result = jnp.where(i == n, jnp.int32(value), result)
    return result


def load_keys(own_ref, par_ref, kz, vz, kt):
    half = own_ref.shape[0]
    lane = lax.broadcasted_iota(jnp.int32, (half, WIN), 1)
    one = lax.broadcasted_iota(jnp.int32, (DK, WIN), 0)
    column = lax.broadcasted_iota(jnp.int32, (DK, WIN), 1)
    for side, ref in enumerate((own_ref, par_ref)):
        at = side * half
        for group in range(GROUPS):
            first = 0 if group == 0 else WIN - DK
            keep = (lane >= first) & (lane < first + DK)
            lo = group * LANES
            vlo = 3 * LANES + lo
            k = jnp.where(keep, ref[:, lo:lo + WIN], jnp.zeros((), jnp.bfloat16))
            kz[group, at:at + half, :] = k
            vz[group, at:at + half, :] = ref[:, vlo:vlo + DV]
            turn = jnp.where(column == one + first, 1.0, 0.0).astype(jnp.bfloat16)
            kt[group, :, at:at + half] = dot(turn, k, NT).astype(jnp.bfloat16)


def group_terms(group, h, q_at, per_owner, q_ref, do_ref, mask_ref, lse_ref, delta_ref, kz, vz):
    rows = per_owner * q_ref.shape[1]
    lo = group * LANES
    q = q_ref[pl.ds(q_at, per_owner), :, lo:lo + WIN].reshape(rows, WIN)
    do = do_ref[pl.ds(h, per_owner), :, lo:lo + DV].reshape(rows, DV)
    lse = jnp.concatenate([lse_ref[group, pl.ds(h + j, 1), :] for j in range(per_owner)], axis=1) * LOG2E
    delta = jnp.concatenate([delta_ref[group, pl.ds(h + j, 1), :] for j in range(per_owner)], axis=1)
    s = dot(kz[group], q, NT)
    dp = dot(vz[group], do, NT)
    p = jnp.exp2(s * (SCALE * LOG2E) - lse) * jnp.concatenate([mask_ref[...]] * per_owner, axis=1)
    ds = (p * (dp - delta)).astype(jnp.bfloat16)
    return q, do, p.astype(jnp.bfloat16), ds


def far_kernel(q_ref, do_ref, lse_ref, delta_ref, seen_ref, own_ref, par_ref,
               right, left, mask_ref, kz, vz, kt, held):
    per_owner, _, count = right.shape
    me = lax.axis_index("ka")
    block = lax.broadcasted_iota(jnp.int32, (seen_ref.shape[0], LANES), 0)
    lane = lax.broadcasted_iota(jnp.int32, (seen_ref.shape[0], LANES), 1)
    select = jnp.where(block == lane // QBLK, 1.0, 0.0)
    mask_ref[...] = dot(seen_ref[...], select, TN)
    load_keys(own_ref, par_ref, kz, vz, kt)

    def one(i, carry):
        h = per_owner * lax.rem(me + pick(i, FAR), KA)
        for group in range(GROUPS):
            ds = group_terms(
                group, h, per_owner * i, per_owner, q_ref, do_ref, mask_ref, lse_ref, delta_ref, kz, vz)[3]
            dqt = dot(kt[group], ds, NN) * SCALE
            for j in range(per_owner):
                held[i, j, group * DK:(group + 1) * DK, :] = dqt[:, j * count:(j + 1) * count].astype(held.dtype)
        return carry

    lax.fori_loop(0, len(FAR), one, 0)
    width = GROUPS * DK
    right[:, :width, :] = held[0]
    left[:, :width, :] = held[1]
    right[:, width:, :] = held[2, :, :DK, :]
    left[:, width:, :] = held[2, :, DK:, :]


def near_kernel(q_ref, do_ref, lse_ref, delta_ref, mask_ref, kz, vz, kt, near, own_out, par_out, acc_k, acc_v):
    _, per_owner, _, count = near.shape
    half = own_out.shape[0]
    me = lax.axis_index("ka")
    steps = NEAR + FAR
    acc_k[...] = jnp.zeros_like(acc_k)
    acc_v[...] = jnp.zeros_like(acc_v)

    def one(i, query_grads):
        h = per_owner * lax.rem(me + pick(i, steps), KA)
        for group in range(GROUPS):
            q, do, p, ds = group_terms(group, h, h, per_owner, q_ref, do_ref, mask_ref, lse_ref, delta_ref, kz, vz)
            acc_v[group] += dot(p, do, NN)
            acc_k[group] += dot(ds, q, NN)
            if query_grads:
                dqt = dot(kt[group], ds, NN) * SCALE
                for j in range(per_owner):
                    near[i, j, group * DK:(group + 1) * DK, :] = dqt[:, j * count:(j + 1) * count]

    def near_one(i, carry):
        one(i, True)
        return carry

    def far_one(i, carry):
        one(i, False)
        return carry

    lax.fori_loop(0, len(NEAR), near_one, 0)
    lax.fori_loop(len(NEAR), KA, far_one, 0)
    low = lax.broadcasted_iota(jnp.int32, (half, LANES), 1) < DK - LANES
    for side, out in enumerate((own_out, par_out)):
        at = side * half
        a = acc_k[0, at:at + half, :] * SCALE
        b = acc_k[1, at:at + half, :] * SCALE
        out[:, :LANES] = a[:, :LANES].astype(out.dtype)
        out[:, LANES:2 * LANES] = jnp.where(low, a[:, LANES:], b[:, :LANES]).astype(out.dtype)
        out[:, 2 * LANES:3 * LANES] = b[:, LANES:].astype(out.dtype)
        for group in range(GROUPS):
            vlo = (3 + group) * LANES
            out[:, vlo:vlo + DV] = acc_v[group, at:at + half, :].astype(out.dtype)


def grads(kernel, rows, keys, matmuls, outs, scratch, *args):
    terms = GROUPS * rows * keys
    return pl.pallas_call(
        kernel,
        out_shape=outs,
        in_specs=[VMEM] * len(args),
        out_specs=tuple(VMEM for _ in outs),
        scratch_shapes=scratch,
        cost_estimate=pl.CostEstimate(flops=2 * terms * matmuls, bytes_accessed=6_000_000, transcendentals=terms),
        compiler_params=pltpu.CompilerParams(vmem_limit_bytes=GRANT),
    )(*args)


def small(kernel, outs, *args):
    return pl.pallas_call(
        kernel,
        out_shape=outs,
        in_specs=[VMEM] * len(args),
        out_specs=tuple(VMEM for _ in outs),
        compiler_params=pltpu.CompilerParams(vmem_limit_bytes=GRANT),
    )(*args)


def copies_kernel(keys, values, out, held, sems):
    width = keys.shape[1]
    parts = (
        pltpu.make_async_copy(keys, held.at[:, pl.ds(0, width)], sems.at[0]),
        pltpu.make_async_copy(values, held.at[:, pl.ds(width, values.shape[1])], sems.at[1]),
    )
    for copy in parts:
        copy.start()
    for copy in parts:
        copy.wait()
    sends = [pltpu.make_async_copy(held, out.at[i], sems.at[2 + i]) for i in range(out.shape[0])]
    for copy in sends:
        copy.start()
    for copy in sends:
        copy.wait()


def message_kernel(near, from_left, from_right, up2, down2, up1, down1):
    f32, bf16 = jnp.float32, jnp.bfloat16
    width = up1.shape[1]
    up1[...] = (near[1] + from_left[:, :width, :].astype(f32)).astype(bf16)
    down1[...] = (near[2] + from_right[:, :width, :].astype(f32)).astype(bf16)
    up2[:, :DK, :] = (near[3, :, :DK, :] + from_left[:, width:, :].astype(f32)).astype(bf16)
    up2[:, DK:, :] = near[3, :, DK:, :].astype(bf16)
    down2[:, :DK, :] = near[4, :, :DK, :].astype(bf16)
    down2[:, DK:, :] = (near[4, :, DK:, :] + from_right[:, width:, :].astype(f32)).astype(bf16)


def finish_kernel(near, a, b, c, d, pieces, dq, dk, dv):
    f32 = jnp.float32
    for j in range(near.shape[1]):
        total = near[0, j] + ((a[j].astype(f32) + b[j].astype(f32)) + (c[j].astype(f32) + d[j].astype(f32)))
        dq[j] = total.T
    kv = pieces[0].astype(f32)
    for i in range(1, pieces.shape[0]):
        kv = kv + pieces[i].astype(f32)
    width = dk.shape[1]
    dk[...] = kv[:, :width]
    dv[...] = kv[:, width:]


def per_device(queries, comp_keys, comp_values, outputs, grad_out, log_sums, visible):
    pb = lax.axis_size("pb")
    ka = lax.axis_size("ka")
    chips = pb // 2
    core = lax.rem(lax.axis_index("pb"), 2)
    same_core = [[2 * i + c for i in range(chips)] for c in range(2)]
    other_core = [(i, i ^ 1) for i in range(pb)]
    rows, width = comp_keys.shape
    both = width + comp_values.shape[1]
    heads, count, _ = queries.shape
    per_owner = heads // ka
    keys = 2 * chips * rows
    half = keys // 2
    f32, bf16 = jnp.float32, jnp.bfloat16
    shape = jax.ShapeDtypeStruct

    def along(x, step):
        return lax.ppermute(x, "ka", [(i, (i + step) % ka) for i in range(ka)])

    copies = pl.pallas_call(
        copies_kernel,
        out_shape=shape((chips, rows, both), bf16),
        in_specs=[HBM, HBM],
        out_specs=HBM,
        scratch_shapes=[pltpu.VMEM((rows, both), bf16), pltpu.SemaphoreType.DMA((2 + chips,))],
        compiler_params=pltpu.CompilerParams(vmem_limit_bytes=COPIES_GRANT),
        name="copies",
    )(comp_keys, comp_values)
    own = lax.all_to_all(copies, "pb", 0, 0, axis_index_groups=same_core, tiled=True).reshape(half, both)
    delta = jnp.stack([
        jnp.sum(
            grad_out[:, :, g * DV:(g + 1) * DV].astype(f32) * outputs[:, :, g * DV:(g + 1) * DV].astype(f32), axis=2
        )
        for g in range(GROUPS)
    ])
    seen = visible.reshape(visible.shape[0], chips, 2, rows)
    seen = jnp.where(core == 0, seen, seen[:, :, ::-1])
    seen = seen.transpose(0, 2, 1, 3).reshape(visible.shape[0], keys).astype(f32)
    seen = jnp.pad(seen, ((0, 8 - seen.shape[0]), (0, 0)))
    me = lax.axis_index("ka")
    far_q = jnp.concatenate([
        lax.dynamic_slice_in_dim(queries, per_owner * lax.rem(me + step, ka), per_owner, 0) for step in FAR
    ])
    own, delta, seen, far_q = lax.optimization_barrier((own, delta, seen, far_q))
    par = lax.ppermute(own, "pb", other_core)

    args = (grad_out, log_sums, delta)
    hops = shape((per_owner, width + DK, count), bf16)
    chunk = (per_owner, width, count)
    right, left, mask, kz, vz, kt = grads(
        far_kernel, len(FAR) * per_owner * count, keys, 2 * DK + DV,
        (
            hops, hops, shape((keys, LANES), f32), shape((GROUPS, keys, WIN), bf16), shape((GROUPS, keys, DV), bf16),
            shape((GROUPS, DK, keys), bf16),
        ),
        [pltpu.VMEM((len(FAR), *chunk), bf16)], far_q, *args, seen, own, par,
    )
    from_left = along(right, 2)
    from_right = along(left, -2)
    near, own_kv, par_kv = grads(
        near_kernel, heads * count, keys, 3 * DK + 2 * DV,
        (shape((len(NEAR), *chunk), f32), shape((half, both), f32), shape((half, both), bf16)),
        [pltpu.VMEM((GROUPS, keys, WIN), f32), pltpu.VMEM((GROUPS, keys, DV), f32)], queries, *args, mask, kz, vz, kt,
    )
    from_other = lax.ppermute(par_kv, "pb", other_core)

    up2, down2, up1, down1 = small(message_kernel, (shape(chunk, bf16),) * 4, near, from_left, from_right)
    from_up2 = along(up2, 2)
    from_down2 = along(down2, -2)
    from_up1 = along(up1, 1)
    from_down1 = along(down1, -1)
    chip_sum = (own_kv + from_other.astype(f32)).astype(bf16)
    pieces = lax.all_to_all(chip_sum.reshape(chips, rows, both), "pb", 0, 0, axis_index_groups=same_core, tiled=True)
    arrived = (from_up2, from_down2, from_up1, from_down1)
    return small(
        finish_kernel,
        (shape((per_owner, count, width), f32), shape((rows, width), f32), shape((rows, both - width), f32)),
        near, *arrived, pieces,
    )


def solution(mesh):
    return jax.shard_map(
        per_device,
        mesh=mesh,
        in_specs=(
            P(None, "pb", "ga"),
            P(("ka", "pb"), "ga"),
            P(("ka", "pb"), "ga"),
            P(None, "pb", "ga"),
            P(None, "pb", "ga"),
            P("ga", None, "pb"),
            P("pb", "ka"),
        ),
        out_specs=(P("ka", "pb", "ga"), P(("ka", "pb"), "ga"), P(("ka", "pb"), "ga")),
        check_vma=False,
    )
```
